32 devices in a mesh: region: 8 (over y, x, core), patch: 4 (over z).
Axes of the slice: x: 2, y: 2, z: 4, core: 2. Of those that a mesh axis runs over, the one named last changes fastest.
Arguments:
- nodes: bfloat16 [8192, 512], P(('region', 'patch')), may hold values from -6 to 6
- edges: bfloat16 [65536, 512], P(('region', 'patch')), may hold values from -6 to 6
- senders: int32 [65536], P(('region', 'patch')), may hold values from 0 to 799, as said below
- receivers: int32 [65536], P(('region', 'patch')), may hold values from 0 to 767, as said below
- valid_counts: int32 [32], P(('region', 'patch')), may hold values from 512 to 2048, as said below
- hub_owner: int32 [2, 8], P(None, 'region'), may hold values from 0 to 3
- edge_in: bfloat16 [2, 3, 512, 512], replicated, may hold values from -0.15625 to 0.15625
- edge_bias: float32 [2, 512], replicated, may hold values from -3 to 3
- edge_out: bfloat16 [2, 512, 512], replicated, may hold values from -0.25 to 0.25
- edge_gain: float32 [2, 512], replicated, may hold values from 0.25 to 1.75
- edge_shift: float32 [2, 512], replicated, may hold values from -2 to 2
- node_in: bfloat16 [2, 2, 512, 512], replicated, may hold values from -0.1875 to 0.1875
- node_bias: float32 [2, 512], replicated, may hold values from -3 to 3
- node_out: bfloat16 [2, 512, 512], replicated, may hold values from -0.25 to 0.25
- node_gain: float32 [2, 512], replicated, may hold values from 0.25 to 1.75
- node_shift: float32 [2, 512], replicated, may hold values from -2 to 2
Outputs:
- nodes_out: bfloat16 [8192, 512], P(('region', 'patch'))
- edges_out: bfloat16 [65536, 512], P(('region', 'patch'))
The draws below stay inside these ranges and needn't reach their ends.
Inputs may be any that keep to these rules, and one draw needn't show every extreme that they name: `senders`: codes below 256 name a row of the previous patch, below 512 of the own patch, below 768 of the next patch, the rest a hub row. `receivers`: codes below 256 name a row of the previous patch, below 512 of the own patch, the rest of the next patch. `valid_counts`: live slots are the first ones of a patch; some patch has all 2048 slots live.
All inputs are finite; a program needn't handle non-finite values.
Results may differ from the reference program's by a relative error of at most 0.012.
Values may be sent and summed in bfloat16 or wider, within the bound.
No kernel may reach another device: no remote copies, remote signals or barrier semaphores. Data moves between devices by JAX's collectives and lax.ppermute only.
A program may use at most 64 MiB of HBM per device.

```python
import jax
import jax.numpy as jnp
from jax import lax

D = 512
NODE_DEV = 256
EDGE_DEV = 2048
HUB = 32
LAYERS = 2
NODES = 8192
EDGES = 65536
N_REGION = 8
N_PATCH = 4


def draw_senders(key, part):
    kinds = jax.random.randint(jax.random.fold_in(key, 11), (EDGES,), 0, 20)
    offset = jax.random.randint(jax.random.fold_in(key, 12), (EDGES,), 0, NODE_DEV)
    hub_pick = jax.random.randint(jax.random.fold_in(key, 13), (EDGES,), 0, HUB)
    codes = jnp.where(kinds < 4, offset, jnp.where(kinds < 10, NODE_DEV + offset, jnp.where(kinds < 14, 2 * NODE_DEV + offset, 3 * NODE_DEV + hub_pick)))
    return codes.astype(jnp.int32)


def draw_receivers(key, part):
    kinds = jax.random.randint(jax.random.fold_in(key, 21), (EDGES,), 0, 16)
    offset = jax.random.randint(jax.random.fold_in(key, 22), (EDGES,), 0, NODE_DEV)
    codes = jnp.where(kinds < 4, offset, jnp.where(kinds < 12, NODE_DEV + offset, 2 * NODE_DEV + offset))
    return codes.astype(jnp.int32)


def draw_valid_counts(key, part):
    total = N_REGION * N_PATCH
    counts = jax.random.randint(jax.random.fold_in(key, 31), (total,), EDGE_DEV // 4, EDGE_DEV + 1)
    fullest = jax.random.randint(jax.random.fold_in(key, 32), (), 0, total)
    return jnp.where(jnp.arange(total) == fullest, EDGE_DEV, counts).astype(jnp.int32)


def touch_ends(drawn, own_key, least, high):
    dims = drawn.shape
    spot = [jax.random.randint(jax.random.fold_in(own_key, axis), (), 0, dims[axis]) for axis in range(len(dims))]
    drawn = drawn.at[tuple(spot)].set(least)
    longest = dims.index(max(dims))
    spot[longest] = (spot[longest] + 1) % dims[longest]
    return drawn.at[tuple(spot)].set(high)


def level_of(stream_key, extent, pieces, least, largest):
    factor_of = 1.0
    for dim, parts in pieces:
        heights = jax.random.uniform(jax.random.fold_in(jax.random.fold_in(stream_key, 6), dim), (parts,), jnp.float32, least / len(pieces), largest / len(pieces))
        factor_of = factor_of * jnp.repeat(jnp.exp(heights), extent[dim] // parts).reshape((-1,) + (1,) * (len(extent) - 1 - dim))
    return factor_of


def scatter_about(own_key, extent, scale, reach, shards=(), kind=jnp.bfloat16):
    result = jax.random.normal(own_key, extent, jnp.float32) * scale
    if len(shards) > 0:
        result = level_of(own_key, extent, shards, -0.22, 0.18) * result
    return jnp.clip(result, min=-reach, max=reach).astype(kind)


def setup_inputs(seed: int = 0) -> dict:
    key_of = jax.random.split(jax.random.key(seed), 17)
    return {
        "nodes": scatter_about(key_of[0], (NODES, D), 1.0, 6.0, ((0, 32),)),
        "edges": scatter_about(key_of[1], (EDGES, D), 1.0, 6.0, ((0, 32),)),
        "senders": draw_senders(jax.random.fold_in(key_of[16], 71), 0),
        "receivers": draw_receivers(jax.random.fold_in(key_of[16], 71), 0),
        "valid_counts": draw_valid_counts(jax.random.fold_in(key_of[16], 71), 0),
        "hub_owner": touch_ends(jax.random.randint(key_of[5], (LAYERS, N_REGION), 0, N_PATCH), jax.random.fold_in(key_of[5], 1), 0, N_PATCH - 1).astype(jnp.int32),
        "edge_in": scatter_about(key_of[6], (LAYERS, 3, D, D), (3 * D) ** -0.5, 0.15625),
        "edge_bias": scatter_about(key_of[7], (LAYERS, D), 0.5, 3.0, (), jnp.float32),
        "edge_out": scatter_about(key_of[8], (LAYERS, D, D), D ** -0.5, 0.25),
        "edge_gain": jnp.clip(1.0 + 0.15 * jax.random.normal(key_of[9], (LAYERS, D), jnp.float32), 0.25, 1.75),
        "edge_shift": scatter_about(key_of[10], (LAYERS, D), 0.3, 2.0, (), jnp.float32),
        "node_in": scatter_about(key_of[11], (LAYERS, 2, D, D), (2 * D) ** -0.5, 0.1875),
        "node_bias": scatter_about(key_of[12], (LAYERS, D), 0.5, 3.0, (), jnp.float32),
        "node_out": scatter_about(key_of[13], (LAYERS, D, D), D ** -0.5, 0.25),
        "node_gain": jnp.clip(1.0 + 0.15 * jax.random.normal(key_of[14], (LAYERS, D), jnp.float32), 0.25, 1.75),
        "node_shift": scatter_about(key_of[15], (LAYERS, D), 0.3, 2.0, (), jnp.float32),
    }


epsilon = 1e-05

def activate(value):
    return value / (1.0 + jnp.exp(-value))

def layer_norm(value, gain, shift):
    center = value - lax.optimization_barrier(jnp.mean(value, axis=-1, keepdims=True))
    spread = lax.optimization_barrier(jnp.mean(center * center, axis=-1, keepdims=True))
    return center * lax.rsqrt(spread + epsilon) * gain + shift

def locate(codes, device_id, hub_device):
    region_id = device_id // N_PATCH
    patch_id = device_id % N_PATCH
    before_dev = region_id * N_PATCH + (patch_id + N_PATCH - 1) % N_PATCH
    after_dev = region_id * N_PATCH + (patch_id + 1) % N_PATCH
    found = jnp.where(codes < NODE_DEV, before_dev * NODE_DEV + codes, jnp.where(codes < 2 * NODE_DEV, device_id * NODE_DEV + codes - NODE_DEV, jnp.where(codes < 3 * NODE_DEV, after_dev * NODE_DEV + codes - 2 * NODE_DEV, hub_device * NODE_DEV + codes - 3 * NODE_DEV)))
    return found.astype(jnp.int32)

def reference(nodes, edges, senders, receivers, valid_counts, hub_owner, edge_in, edge_bias, edge_out, edge_gain, edge_shift, node_in, node_bias, node_out, node_gain, node_shift):
    positions = jnp.arange(EDGES, dtype=jnp.int32)
    device_id = (positions // EDGE_DEV).astype(jnp.int32)
    region_id = (device_id // N_PATCH).astype(jnp.int32)
    is_valid = positions % EDGE_DEV < jnp.take(valid_counts, device_id)
    recv_index = locate(receivers, device_id, device_id)
    for layer_index in range(LAYERS):
        hub_device = region_id * N_PATCH + jnp.take(hub_owner[layer_index], region_id)
        send_index = locate(senders, device_id, hub_device)
        send_proj = jnp.dot(nodes, edge_in[layer_index, 1], preferred_element_type=jnp.float32).astype(jnp.bfloat16)
        recv_proj = jnp.dot(nodes, edge_in[layer_index, 2], preferred_element_type=jnp.float32).astype(jnp.bfloat16)
        pre_edge = jnp.dot(edges, edge_in[layer_index, 0], preferred_element_type=jnp.float32)
        pre_edge = pre_edge + jnp.take(send_proj, send_index, axis=0).astype(jnp.float32)
        pre_edge = pre_edge + jnp.take(recv_proj, recv_index, axis=0).astype(jnp.float32)
        pre_edge = pre_edge + edge_bias[layer_index]
        activated = activate(pre_edge).astype(jnp.bfloat16)
        mixed = jnp.dot(activated, edge_out[layer_index], preferred_element_type=jnp.float32)
        updated = edges.astype(jnp.float32) + layer_norm(mixed, edge_gain[layer_index], edge_shift[layer_index])
        edges = jnp.where(is_valid[:, None], updated, 0.0).astype(jnp.bfloat16)
        aggregate = jax.ops.segment_sum(edges.astype(jnp.float32), recv_index, num_segments=NODES).astype(jnp.bfloat16)
        pre_node = jnp.dot(nodes, node_in[layer_index, 0], preferred_element_type=jnp.float32)
        pre_node = pre_node + jnp.dot(aggregate, node_in[layer_index, 1], preferred_element_type=jnp.float32)
        pre_node = pre_node + node_bias[layer_index]
        node_act = activate(pre_node).astype(jnp.bfloat16)
        node_mixed = jnp.dot(node_act, node_out[layer_index], preferred_element_type=jnp.float32)
        nodes = (nodes.astype(jnp.float32) + layer_norm(node_mixed, node_gain[layer_index], node_shift[layer_index])).astype(jnp.bfloat16)
    return (nodes, edges)
```

```python
import functools

import jax
import jax.numpy as jnp
from jax import lax
from jax.experimental import pallas as pl
from jax.experimental.pallas import tpu as pltpu
from jax.sharding import PartitionSpec as P

HUB = 32
LAYERS = 2
LANES = 128

epsilon = 1e-05

F32 = jnp.float32
BF16 = jnp.bfloat16


def from_behind(block, axis, distance):
    size = lax.axis_size(axis)
    return lax.ppermute(block, axis, [((i - distance) % size, i) for i in range(size)])


def dot(left, right):
    return jnp.dot(left, right, preferred_element_type=F32)


def silu(value):
    half = value * 0.5
    return half + half * jnp.tanh(half)


def layer_norm(value, gain, shift):
    center = value - jnp.mean(value, axis=-1, keepdims=True)
    spread = jnp.mean(center * center, axis=-1, keepdims=True)
    return center * lax.rsqrt(spread + epsilon) * gain + shift


def columns_of(codes_ref, first, count):
    rows = [
        jnp.broadcast_to(codes_ref[pl.ds(first + i, 1), :], (LANES, LANES)).T
        for i in range(count)
    ]
    return jnp.concatenate(rows, axis=0)


def one_hot(codes, start, width):
    lane = lax.broadcasted_iota(jnp.int32, codes.shape, 1)
    offset = codes - lane
    parts = [
        jnp.where(offset == start + t * LANES, 1.0, 0.0).astype(BF16)
        for t in range(width // LANES)
    ]
    return jnp.concatenate(parts, axis=1)


def one_hot_rows(codes_ref, first, count, width):
    parts = []
    for i in range(count):
        row = codes_ref[pl.ds(first + i, 1), :]
        sub = lax.broadcasted_iota(jnp.int32, (width, LANES), 0)
        parts.append(jnp.where(sub == row, 1.0, 0.0).astype(BF16))
    return jnp.concatenate(parts, axis=1)


def linear_kernel(layer, edges_ref, weight_ref, bias_ref, out_ref):
    out_ref[...] = dot(edges_ref[...], weight_ref[0, 0]) + bias_ref[layer : layer + 1, :]


def own_kernel(rows, fused, layer, *refs):
    if fused:
        (send_ref, recv_ref, edges_ref, first_ref, bias_ref, nodes_ref, ws_ref, wr_ref) = refs[:8]
    else:
        (send_ref, recv_ref, pre_ref, nodes_ref, ws_ref, wr_ref) = refs[:6]
    out_ref, table_ref = refs[-2:]
    step = pl.program_id(0)

    @pl.when(step == 0)
    def _():
        own = nodes_ref[...]
        table_ref[:rows, :] = dot(own, ws_ref[0, 0]).astype(BF16)
        table_ref[rows:, :] = dot(own, wr_ref[0, 0]).astype(BF16)

    count = out_ref.shape[0] // LANES
    picks = jnp.concatenate(
        [
            one_hot(columns_of(send_ref, step * count, count), rows, rows),
            one_hot(columns_of(recv_ref, step * count, count), rows, rows),
        ],
        axis=1,
    )
    total = dot(picks, table_ref[...])
    if fused:
        total = total + dot(edges_ref[...], first_ref[0, 0]) + bias_ref[layer : layer + 1, :]
    else:
        total = total + pre_ref[...]
    out_ref[...] = total


def edge_kernel(
    rows,
    layer,
    size,
    valid_ref,
    owner_ref,
    send_ref,
    recv_ref,
    edges_ref,
    pre_ref,
    own_ref,
    prev_ref,
    next_ref,
    far_ref,
    ws_ref,
    wr_ref,
    wo_ref,
    gain_ref,
    shift_ref,
    out_ref,
    to_prev_ref,
    kept_ref,
    to_next_ref,
    table_ref,
    total_ref,
):
    step = pl.program_id(0)

    @pl.when(step == 0)
    def _():
        weight_s = ws_ref[0, 0]
        weight_r = wr_ref[0, 0]
        before = prev_ref[...]
        after = next_ref[...]
        table_ref[0 * rows : 1 * rows, :] = dot(before, weight_s).astype(BF16)
        table_ref[1 * rows : 2 * rows, :] = dot(after, weight_s).astype(BF16)
        table_ref[2 * rows : 3 * rows, :] = dot(before, weight_r).astype(BF16)
        table_ref[3 * rows : 4 * rows, :] = dot(after, weight_r).astype(BF16)
        away = owner_ref[layer, 0] - lax.axis_index("patch")
        away = jnp.where(away < 0, away + size, away)
        hub = own_ref[:HUB, :]
        if size > 3:
            spot = jnp.clip(away - 2, 0, size - 4)
            hub = jnp.where(away > 1, far_ref[pl.ds(pl.multiple_of(spot * HUB, HUB), HUB), :], hub)
        hub = jnp.where(away == size - 1, prev_ref[:HUB, :], hub)
        hub = jnp.where(away == 1, next_ref[:HUB, :], hub)
        hub = jnp.where(away == 0, own_ref[:HUB, :], hub)
        table_ref[4 * rows : 4 * rows + HUB, :] = dot(hub, weight_s).astype(BF16)
        table_ref[4 * rows + HUB :, :] = jnp.zeros_like(table_ref[4 * rows + HUB :, :])
        total_ref[...] = jnp.zeros_like(total_ref)

    block = out_ref.shape[0]
    count = block // LANES
    send = columns_of(send_ref, step * count, count)
    recv = columns_of(recv_ref, step * count, count)
    picks = jnp.concatenate(
        [
            one_hot(send, 0, rows),
            one_hot(send, 2 * rows, rows),
            one_hot(recv, 0, rows),
            one_hot(recv, 2 * rows, rows),
            one_hot(send, 3 * rows, LANES),
        ],
        axis=1,
    )
    activated = silu(pre_ref[...] + dot(picks, table_ref[...])).astype(BF16)
    mixed = dot(activated, wo_ref[0])
    normed = layer_norm(mixed, gain_ref[layer : layer + 1, :], shift_ref[layer : layer + 1, :])
    spot = step * block + lax.broadcasted_iota(jnp.int32, (block, 1), 0)
    updated = jnp.where(spot < valid_ref[0], edges_ref[...].astype(F32) + normed, 0.0).astype(BF16)
    out_ref[...] = updated
    total_ref[...] += dot(one_hot_rows(recv_ref, step * count, count, 3 * rows), updated)

    @pl.when(step == pl.num_programs(0) - 1)
    def _():
        to_prev_ref[...] = total_ref[:rows, :].astype(BF16)
        kept_ref[...] = total_ref[rows : 2 * rows, :]
        to_next_ref[...] = total_ref[2 * rows :, :].astype(BF16)


def node_kernel(
    layer,
    nodes_ref,
    kept_ref,
    from_prev_ref,
    from_next_ref,
    wh_ref,
    wa_ref,
    bias_ref,
    wo_ref,
    gain_ref,
    shift_ref,
    out_ref,
):
    nodes = nodes_ref[...]
    summed = from_prev_ref[...].astype(F32) + kept_ref[...] + from_next_ref[...].astype(F32)
    pre_node = dot(nodes, wh_ref[0, 0]) + dot(summed.astype(BF16), wa_ref[0, 0])
    pre_node = pre_node + bias_ref[layer : layer + 1, :]
    mixed = dot(silu(pre_node).astype(BF16), wo_ref[0])
    normed = layer_norm(mixed, gain_ref[layer : layer + 1, :], shift_ref[layer : layer + 1, :])
    out_ref[...] = (nodes.astype(F32) + normed).astype(BF16)


def whole(shape):
    return pl.BlockSpec(shape, lambda *_: (0,) * len(shape))


def picked(shape, spot):
    block = (1,) * len(spot) + shape[len(spot) :]
    index = tuple(spot) + (0,) * (len(shape) - len(spot))
    return pl.BlockSpec(block, lambda *_: index)


def scalars():
    return pl.BlockSpec(memory_space=pltpu.SMEM)


def cost(flops, moved):
    return pl.CostEstimate(flops=flops, bytes_accessed=moved, transcendentals=0)


def local(
    nodes,
    edges,
    senders,
    receivers,
    valid_counts,
    hub_owner,
    edge_in,
    edge_bias,
    edge_out,
    edge_gain,
    edge_shift,
    node_in,
    node_bias,
    node_out,
    node_gain,
    node_shift,
):
    rows, width = nodes.shape
    slots = edges.shape[0]
    size = lax.axis_size("patch")
    block = min(512, slots)
    steps = slots // block
    send = senders.reshape(slots // LANES, LANES)
    recv = receivers.reshape(slots // LANES, LANES)
    by_block = pl.BlockSpec((block, width), lambda i: (i, 0))
    square = 2 * slots * width * width
    pre = None
    for layer in range(LAYERS):
        from_prev = from_behind(nodes, "patch", 1)
        from_next = from_behind(nodes, "patch", -1)
        top = nodes[:HUB]
        far = [from_behind(top, "patch", -d) for d in range(2, size - 1)]
        far = jnp.concatenate(far, axis=0) if len(far) > 1 else (far[0] if far else top)
        w0 = picked(edge_in.shape, (layer, 0))
        ws = picked(edge_in.shape, (layer, 1))
        wr = picked(edge_in.shape, (layer, 2))
        fused = pre is None
        if fused:
            head = (edges, edge_in, edge_bias)
            head_specs = [by_block, w0, whole(edge_bias.shape)]
        else:
            head = (pre,)
            head_specs = [by_block]
        pre = pl.pallas_call(
            functools.partial(own_kernel, rows, fused, layer),
            out_shape=jax.ShapeDtypeStruct((slots, width), F32),
            grid=(steps,),
            in_specs=[whole(send.shape), whole(recv.shape)]
            + head_specs
            + [whole(nodes.shape), ws, wr],
            out_specs=by_block,
            scratch_shapes=[pltpu.VMEM((2 * rows, width), BF16)],
            cost_estimate=cost(square * (2 if fused else 1), 6 * slots * width),
            name="own_part",
        )(send, recv, *head, nodes, edge_in, edge_in)
        edges, to_prev, kept, to_next = pl.pallas_call(
            functools.partial(edge_kernel, rows, layer, size),
            out_shape=(
                jax.ShapeDtypeStruct((slots, width), BF16),
                jax.ShapeDtypeStruct((rows, width), BF16),
                jax.ShapeDtypeStruct((rows, width), F32),
                jax.ShapeDtypeStruct((rows, width), BF16),
            ),
            grid=(steps,),
            in_specs=[
                scalars(),
                scalars(),
                whole(send.shape),
                whole(recv.shape),
                by_block,
                by_block,
                whole(nodes.shape),
                whole(nodes.shape),
                whole(nodes.shape),
                whole(far.shape),
                ws,
                wr,
                picked(edge_out.shape, (layer,)),
                whole(edge_gain.shape),
                whole(edge_shift.shape),
            ],
            out_specs=(by_block,) + (whole((rows, width)),) * 3,
            scratch_shapes=[
                pltpu.VMEM((4 * rows + LANES, width), BF16),
                pltpu.VMEM((3 * rows, width), F32),
            ],
            cost_estimate=cost(6 * square, 8 * slots * width),
            name="edge_part",
        )(
            valid_counts,
            hub_owner,
            send,
            recv,
            edges,
            pre,
            nodes,
            from_prev,
            from_next,
            far,
            edge_in,
            edge_in,
            edge_out,
            edge_gain,
            edge_shift,
        )
        sum_next = from_behind(to_prev, "patch", -1)
        sum_prev = from_behind(to_next, "patch", 1)
        if layer + 1 < LAYERS:
            pre = pl.pallas_call(
                functools.partial(linear_kernel, layer + 1),
                out_shape=jax.ShapeDtypeStruct((slots, width), F32),
                grid=(steps,),
                in_specs=[
                    by_block,
                    picked(edge_in.shape, (layer + 1, 0)),
                    whole(edge_bias.shape),
                ],
                out_specs=by_block,
                cost_estimate=cost(square, 6 * slots * width),
                name="linear_part",
            )(edges, edge_in, edge_bias)
        nodes = pl.pallas_call(
            functools.partial(node_kernel, layer),
            out_shape=jax.ShapeDtypeStruct((rows, width), BF16),
            grid=(1,),
            in_specs=[whole((rows, width))] * 4
            + [
                picked(node_in.shape, (layer, 0)),
                picked(node_in.shape, (layer, 1)),
                whole(node_bias.shape),
                picked(node_out.shape, (layer,)),
                whole(node_gain.shape),
                whole(node_shift.shape),
            ],
            out_specs=whole((rows, width)),
            cost_estimate=cost(6 * rows * width * width, 2 * width * width * 3),
            name="node_part",
        )(
            nodes,
            kept,
            sum_prev,
            sum_next,
            node_in,
            node_in,
            node_bias,
            node_out,
            node_gain,
            node_shift,
        )
    return (nodes, edges)


def solution(mesh):
    placed = (
        P(("region", "patch"), None),
        P(("region", "patch"), None),
        P(("region", "patch")),
        P(("region", "patch")),
        P(("region", "patch")),
        P(None, "region"),
    ) + (P(),) * 10
    return jax.shard_map(
        local,
        mesh=mesh,
        in_specs=placed,
        out_specs=(P(("region", "patch"), None), P(("region", "patch"), None)),
        check_vma=False,
    )
```

```python
import functools

import jax
import jax.numpy as jnp
from jax import lax
from jax.experimental import pallas as pl
from jax.experimental.pallas import tpu as pltpu
from jax.sharding import PartitionSpec as P

HUB = 32
LAYERS = 2
LANES = 128
GRANT = 24 << 20

epsilon = 1e-05

F32 = jnp.float32
BF16 = jnp.bfloat16


def from_behind(block, axis, distance):
    size = lax.axis_size(axis)
    return lax.ppermute(block, axis, [((i - distance) % size, i) for i in range(size)])


def dot(left, right):
    return jnp.dot(left, right, preferred_element_type=F32)


def silu(value):
    half = value * 0.5
    return half + half * jnp.tanh(half)


def layer_norm(value, gain, shift):
    center = value - jnp.mean(value, axis=-1, keepdims=True)
    spread = jnp.mean(center * center, axis=-1, keepdims=True)
    return center * lax.rsqrt(spread + epsilon) * gain + shift


def columns_of(codes_ref, first, count):
    rows = [
        jnp.broadcast_to(codes_ref[pl.ds(first + i, 1), :], (LANES, LANES)).T
        for i in range(count)
    ]
    return jnp.concatenate(rows, axis=0)


def one_hot(codes, start, width):
    lane = lax.broadcasted_iota(jnp.int32, codes.shape, 1)
    offset = codes - lane
    parts = [
        jnp.where(offset == start + t * LANES, 1.0, 0.0).astype(BF16)
        for t in range(width // LANES)
    ]
    return jnp.concatenate(parts, axis=1)


def one_hot_rows(codes_ref, first, count, width):
    parts = []
    for i in range(count):
        row = codes_ref[pl.ds(first + i, 1), :]
        sub = lax.broadcasted_iota(jnp.int32, (width, LANES), 0)
        parts.append(jnp.where(sub == row, 1.0, 0.0).astype(BF16))
    return jnp.concatenate(parts, axis=1)


def linear_kernel(layer, edges_ref, weight_ref, bias_ref, out_ref):
    out_ref[...] = dot(edges_ref[...], weight_ref[0, 0]) + bias_ref[layer : layer + 1, :]


def own_table(nodes, ws_ref, wr_ref, table_ref):
    rows = nodes.shape[0]
    table_ref[:rows, :] = dot(nodes, ws_ref[0, 0]).astype(BF16)
    table_ref[rows:, :] = dot(nodes, wr_ref[0, 0]).astype(BF16)


def own_picks(send_ref, recv_ref, first, count, rows):
    return jnp.concatenate(
        [
            one_hot(columns_of(send_ref, first, count), rows, rows),
            one_hot(columns_of(recv_ref, first, count), rows, rows),
        ],
        axis=1,
    )


def own_kernel(send_ref, recv_ref, pre_ref, nodes_ref, ws_ref, wr_ref, out_ref, table_ref):
    step = pl.program_id(0)
    rows = nodes_ref.shape[0]

    @pl.when(step == 0)
    def _():
        own_table(nodes_ref[...], ws_ref, wr_ref, table_ref)

    count = out_ref.shape[0] // LANES
    picks = own_picks(send_ref, recv_ref, step * count, count, rows)
    out_ref[...] = pre_ref[...] + dot(picks, table_ref[...])


def first_kernel(
    parity,
    layer,
    steps,
    send_ref,
    recv_ref,
    nodes_ref,
    bias_ref,
    edges_ref,
    weights_ref,
    *refs,
):
    out_ref, table_ref, weight_buf, edges_buf, out_buf, weight_sem, in_sem, out_sem = refs[-8:]
    rows = nodes_ref.shape[0]
    block = edges_buf.shape[0] // steps
    count = block // LANES

    def span(i):
        return pl.ds(i * block, block)

    def fetch(i):
        return pltpu.make_async_copy(edges_ref.at[span(i)], edges_buf.at[span(i)], in_sem.at[i])

    def weight(i):
        return pltpu.make_async_copy(weights_ref.at[layer, i], weight_buf.at[i], weight_sem.at[i])

    def put(i):
        return pltpu.make_async_copy(out_buf.at[span(i)], out_ref.at[span(i)], out_sem.at[i])

    @pl.when(lax.axis_index("region") % 2 == parity)
    def _():
        for i in (1, 2, 0):
            weight(i).start()
        for i in range(steps):
            fetch(i).start()
        weight(1).wait()
        table_ref[:rows, :] = dot(nodes_ref[...], weight_buf[1]).astype(BF16)
        weight(2).wait()
        table_ref[rows:, :] = dot(nodes_ref[...], weight_buf[2]).astype(BF16)
        weight(0).wait()
        for i in range(steps):
            fetch(i).wait()
            picks = own_picks(send_ref, recv_ref, i * count, count, rows)
            total = dot(picks, table_ref[...]) + dot(edges_buf[span(i), :], weight_buf[0])
            out_buf[span(i), :] = total + bias_ref[layer : layer + 1, :]
            put(i).start()
        for i in range(steps):
            put(i).wait()


def edge_kernel(
    rows,
    layer,
    size,
    valid_ref,
    owner_ref,
    send_ref,
    recv_ref,
    edges_ref,
    pre_ref,
    own_ref,
    prev_ref,
    next_ref,
    far_ref,
    ws_ref,
    wr_ref,
    wo_ref,
    gain_ref,
    shift_ref,
    out_ref,
    to_prev_ref,
    kept_ref,
    to_next_ref,
    table_ref,
    total_ref,
):
    step = pl.program_id(0)

    @pl.when(step == 0)
    def _():
        weight_s = ws_ref[0, 0]
        weight_r = wr_ref[0, 0]
        before = prev_ref[...]
        after = next_ref[...]
        table_ref[0 * rows : 1 * rows, :] = dot(before, weight_s).astype(BF16)
        table_ref[1 * rows : 2 * rows, :] = dot(after, weight_s).astype(BF16)
        table_ref[2 * rows : 3 * rows, :] = dot(before, weight_r).astype(BF16)
        table_ref[3 * rows : 4 * rows, :] = dot(after, weight_r).astype(BF16)
        away = owner_ref[layer, 0] - lax.axis_index("patch")
        away = jnp.where(away < 0, away + size, away)
        hub = own_ref[:HUB, :]
        if size > 3:
            spot = jnp.clip(away - 2, 0, size - 4)
            hub = jnp.where(away > 1, far_ref[pl.ds(pl.multiple_of(spot * HUB, HUB), HUB), :], hub)
        hub = jnp.where(away == size - 1, prev_ref[:HUB, :], hub)
        hub = jnp.where(away == 1, next_ref[:HUB, :], hub)
        hub = jnp.where(away == 0, own_ref[:HUB, :], hub)
        table_ref[4 * rows : 4 * rows + HUB, :] = dot(hub, weight_s).astype(BF16)
        table_ref[4 * rows + HUB :, :] = jnp.zeros_like(table_ref[4 * rows + HUB :, :])
        total_ref[...] = jnp.zeros_like(total_ref)

    block = out_ref.shape[0]
    count = block // LANES
    send = columns_of(send_ref, step * count, count)
    recv = columns_of(recv_ref, step * count, count)
    picks = jnp.concatenate(
        [
            one_hot(send, 0, rows),
            one_hot(send, 2 * rows, rows),
            one_hot(recv, 0, rows),
            one_hot(recv, 2 * rows, rows),
            one_hot(send, 3 * rows, LANES),
        ],
        axis=1,
    )
    activated = silu(pre_ref[...] + dot(picks, table_ref[...])).astype(BF16)
    mixed = dot(activated, wo_ref[0])
    normed = layer_norm(mixed, gain_ref[layer : layer + 1, :], shift_ref[layer : layer + 1, :])
    spot = step * block + lax.broadcasted_iota(jnp.int32, (block, 1), 0)
    updated = jnp.where(spot < valid_ref[0], edges_ref[...].astype(F32) + normed, 0.0).astype(BF16)
    out_ref[...] = updated
    total_ref[...] += dot(one_hot_rows(recv_ref, step * count, count, 3 * rows), updated)

    @pl.when(step == pl.num_programs(0) - 1)
    def _():
        to_prev_ref[...] = total_ref[:rows, :].astype(BF16)
        kept_ref[...] = total_ref[rows : 2 * rows, :]
        to_next_ref[...] = total_ref[2 * rows :, :].astype(BF16)


def node_kernel(
    layer,
    nodes_ref,
    kept_ref,
    from_prev_ref,
    from_next_ref,
    wh_ref,
    wa_ref,
    bias_ref,
    wo_ref,
    gain_ref,
    shift_ref,
    *refs,
):
    out_ref = refs[-1]
    nodes = nodes_ref[...]
    summed = from_prev_ref[...].astype(F32) + kept_ref[...] + from_next_ref[...].astype(F32)
    pre_node = dot(nodes, wh_ref[0, 0]) + dot(summed.astype(BF16), wa_ref[0, 0])
    pre_node = pre_node + bias_ref[layer : layer + 1, :]
    mixed = dot(silu(pre_node).astype(BF16), wo_ref[0])
    normed = layer_norm(mixed, gain_ref[layer : layer + 1, :], shift_ref[layer : layer + 1, :])
    out_ref[...] = (nodes.astype(F32) + normed).astype(BF16)


def whole(shape):
    return pl.BlockSpec(shape, lambda *_: (0,) * len(shape))


def picked(shape, spot):
    block = (1,) * len(spot) + shape[len(spot) :]
    index = tuple(spot) + (0,) * (len(shape) - len(spot))
    return pl.BlockSpec(block, lambda *_: index)


def scalars():
    return pl.BlockSpec(memory_space=pltpu.SMEM)


def cost(flops, moved):
    return pl.CostEstimate(flops=flops, bytes_accessed=moved, transcendentals=0)


def local(
    nodes,
    edges,
    senders,
    receivers,
    valid_counts,
    hub_owner,
    edge_in,
    edge_bias,
    edge_out,
    edge_gain,
    edge_shift,
    node_in,
    node_bias,
    node_out,
    node_gain,
    node_shift,
):
    rows, width = nodes.shape
    slots = edges.shape[0]
    size = lax.axis_size("patch")
    block = min(512, slots)
    steps = slots // block
    send = senders.reshape(slots // LANES, LANES)
    recv = receivers.reshape(slots // LANES, LANES)
    by_block = pl.BlockSpec((block, width), lambda i: (i, 0))
    square = 2 * slots * width * width
    def start_edges(parity, held):
        anywhere = pl.BlockSpec(memory_space=pltpu.HBM)
        given = () if held is None else (held,)
        return pl.pallas_call(
            functools.partial(first_kernel, parity, 0, steps),
            out_shape=jax.ShapeDtypeStruct((slots, width), F32),
            in_specs=[whole(send.shape), whole(recv.shape), whole(nodes.shape)]
            + [whole(edge_bias.shape), anywhere, anywhere]
            + [anywhere] * len(given),
            out_specs=anywhere,
            grid=(1,),
            input_output_aliases={6: 0} if given else {},
            scratch_shapes=[
                pltpu.VMEM((2 * rows, width), BF16),
                pltpu.VMEM((3, width, width), BF16),
                pltpu.VMEM((slots, width), BF16),
                pltpu.VMEM((slots, width), F32),
                pltpu.SemaphoreType.DMA((3,)),
                pltpu.SemaphoreType.DMA((steps,)),
                pltpu.SemaphoreType.DMA((steps,)),
            ],
            cost_estimate=cost(2 * square, 6 * slots * width),
            name="first_part",
        )(send, recv, nodes, edge_bias, edges, edge_in, *given)

    early = start_edges(1, None)
    nodes, early = lax.optimization_barrier((nodes, early))
    for layer in range(LAYERS):
        from_prev = from_behind(nodes, "patch", 1)
        from_next = from_behind(nodes, "patch", -1)
        top = nodes[:HUB]
        far = [from_behind(top, "patch", -d) for d in range(2, size - 1)]
        far = jnp.concatenate(far, axis=0) if len(far) > 1 else (far[0] if far else top)
        ws = picked(edge_in.shape, (layer, 1))
        wr = picked(edge_in.shape, (layer, 2))
        if layer == 0:
            pre = start_edges(0, early)
        else:
            pre = pl.pallas_call(
                own_kernel,
                out_shape=jax.ShapeDtypeStruct((slots, width), F32),
                grid=(steps,),
                in_specs=[whole(send.shape), whole(recv.shape), by_block]
                + [whole(nodes.shape), ws, wr],
                out_specs=by_block,
                scratch_shapes=[pltpu.VMEM((2 * rows, width), BF16)],
                compiler_params=pltpu.CompilerParams(vmem_limit_bytes=GRANT),
                cost_estimate=cost(square, 8 * slots * width),
                name="own_part",
            )(send, recv, pre, nodes, edge_in, edge_in)
        edges, to_prev, kept, to_next = pl.pallas_call(
            functools.partial(edge_kernel, rows, layer, size),
            out_shape=(
                jax.ShapeDtypeStruct((slots, width), BF16),
                jax.ShapeDtypeStruct((rows, width), BF16),
                jax.ShapeDtypeStruct((rows, width), F32),
                jax.ShapeDtypeStruct((rows, width), BF16),
            ),
            grid=(steps,),
            in_specs=[
                scalars(),
                scalars(),
                whole(send.shape),
                whole(recv.shape),
                by_block,
                by_block,
                whole(nodes.shape),
                whole(nodes.shape),
                whole(nodes.shape),
                whole(far.shape),
                ws,
                wr,
                picked(edge_out.shape, (layer,)),
                whole(edge_gain.shape),
                whole(edge_shift.shape),
            ],
            out_specs=(by_block,) + (whole((rows, width)),) * 3,
            scratch_shapes=[
                pltpu.VMEM((4 * rows + LANES, width), BF16),
                pltpu.VMEM((3 * rows, width), F32),
            ],
            compiler_params=pltpu.CompilerParams(vmem_limit_bytes=GRANT),
            cost_estimate=cost(6 * square, 8 * slots * width),
            name="edge_part",
        )(
            valid_counts,
            hub_owner,
            send,
            recv,
            edges,
            pre,
            nodes,
            from_prev,
            from_next,
            far,
            edge_in,
            edge_in,
            edge_out,
            edge_gain,
            edge_shift,
        )
        sum_next = from_behind(to_prev, "patch", -1)
        sum_prev = from_behind(to_next, "patch", 1)
        after = ()
        if layer + 1 < LAYERS:
            pre = pl.pallas_call(
                functools.partial(linear_kernel, layer + 1),
                out_shape=jax.ShapeDtypeStruct((slots, width), F32),
                grid=(steps,),
                in_specs=[
                    by_block,
                    picked(edge_in.shape, (layer + 1, 0)),
                    whole(edge_bias.shape),
                ],
                out_specs=by_block,
                compiler_params=pltpu.CompilerParams(vmem_limit_bytes=GRANT),
                cost_estimate=cost(square, 6 * slots * width),
                name="linear_part",
            )(edges, edge_in, edge_bias)
            after = (pre,)
        nodes = pl.pallas_call(
            functools.partial(node_kernel, layer),
            out_shape=jax.ShapeDtypeStruct((rows, width), BF16),
            grid=(1,),
            in_specs=[whole((rows, width))] * 4
            + [
                picked(node_in.shape, (layer, 0)),
                picked(node_in.shape, (layer, 1)),
                whole(node_bias.shape),
                picked(node_out.shape, (layer,)),
                whole(node_gain.shape),
                whole(node_shift.shape),
            ]
            + [pl.BlockSpec(memory_space=pl.ANY)] * len(after),
            out_specs=whole((rows, width)),
            compiler_params=pltpu.CompilerParams(vmem_limit_bytes=GRANT),
            cost_estimate=cost(6 * rows * width * width, 2 * width * width * 3),
            name="node_part",
        )(
            nodes,
            kept,
            sum_prev,
            sum_next,
            node_in,
            node_in,
            node_bias,
            node_out,
            node_gain,
            node_shift,
            *after,
        )
    return (nodes, edges)


def solution(mesh):
    placed = (
        P(("region", "patch"), None),
        P(("region", "patch"), None),
        P(("region", "patch")),
        P(("region", "patch")),
        P(("region", "patch")),
        P(None, "region"),
    ) + (P(),) * 10
    return jax.shard_map(
        local,
        mesh=mesh,
        in_specs=placed,
        out_specs=(P(("region", "patch"), None), P(("region", "patch"), None)),
        check_vma=False,
    )
```

```python
import functools

import jax
import jax.numpy as jnp
from jax import lax
from jax.experimental import pallas as pl
from jax.experimental.pallas import tpu as pltpu
from jax.sharding import PartitionSpec as P

HUB = 32
LAYERS = 2
LANES = 128
GRANT = 24 << 20

epsilon = 1e-05

F32 = jnp.float32
BF16 = jnp.bfloat16


def from_behind(block, axis, distance):
    size = lax.axis_size(axis)
    return lax.ppermute(block, axis, [((i - distance) % size, i) for i in range(size)])


def dot(left, right):
    return jnp.dot(left, right, preferred_element_type=F32)


def silu(value):
    half = value * 0.5
    return half + half * jnp.tanh(half)


def layer_norm(value, gain, shift):
    center = value - jnp.mean(value, axis=-1, keepdims=True)
    spread = jnp.mean(center * center, axis=-1, keepdims=True)
    return center * lax.rsqrt(spread + epsilon) * gain + shift


def selector(codes_ref, first, count, starts):
    groups = []
    for i in range(count):
        row = codes_ref[pl.ds(first + i, 1), :]
        parts = []
        for start, width in starts:
            near = jnp.clip(row - start, -1, width).astype(F32)
            near = jnp.broadcast_to(near, (LANES, LANES)).T.astype(BF16)
            for t in range(width // LANES):
                lane = lax.broadcasted_iota(jnp.int32, (LANES, LANES), 1) + t * LANES
                parts.append(jnp.where(near == lane.astype(BF16), BF16(1), BF16(0)))
        groups.append(jnp.concatenate(parts, axis=1))
    return jnp.concatenate(groups, axis=0)


def selector_rows(codes_ref, first, count, width):
    tile = 2 * LANES
    groups = []
    for i in range(count):
        row = codes_ref[pl.ds(first + i, 1), :]
        parts = []
        for start in range(0, width, tile):
            near = jnp.clip(row - start, -1, tile).astype(F32)
            near = jnp.broadcast_to(near, (tile, LANES)).astype(BF16)
            sub = lax.broadcasted_iota(jnp.int32, (tile, LANES), 0).astype(BF16)
            parts.append(jnp.where(near == sub, BF16(1), BF16(0)))
        groups.append(jnp.concatenate(parts, axis=0))
    return jnp.concatenate(groups, axis=1)


def linear_kernel(layer, edges_ref, weight_ref, bias_ref, out_ref):
    out_ref[...] = dot(edges_ref[...], weight_ref[0, 0]) + bias_ref[layer : layer + 1, :]


def own_table(nodes, ws_ref, wr_ref, table_ref):
    rows = nodes.shape[0]
    table_ref[:rows, :] = dot(nodes, ws_ref[0, 0]).astype(BF16)
    table_ref[rows:, :] = dot(nodes, wr_ref[0, 0]).astype(BF16)


def own_picks(send_ref, recv_ref, first, count, rows):
    spans = tuple((rows + at, 2 * LANES) for at in range(0, rows, 2 * LANES))
    return jnp.concatenate(
        [selector(send_ref, first, count, spans), selector(recv_ref, first, count, spans)],
        axis=1,
    )


def own_sum(step, send_ref, recv_ref, nodes_ref, ws_ref, wr_ref, table_ref, edges):
    rows = nodes_ref.shape[0]

    @pl.when(step == 0)
    def _():
        own_table(nodes_ref[...], ws_ref, wr_ref, table_ref)

    count = edges // LANES
    return dot(own_picks(send_ref, recv_ref, step * count, count, rows), table_ref[...])


def own_kernel(send_ref, recv_ref, nodes_ref, ws_ref, wr_ref, pre_ref, out_ref, table_ref):
    gathered = own_sum(
        pl.program_id(0), send_ref, recv_ref, nodes_ref, ws_ref, wr_ref, table_ref, out_ref.shape[0]
    )
    out_ref[...] = pre_ref[...] + gathered


def is_odd():
    return lax.axis_index("region") % 2 == 1


def first_kernel(late, layer, send_ref, recv_ref, nodes_ref, ws_ref, wr_ref, *refs):
    edges_ref, first_ref, bias_ref = refs[:3]
    out_ref, table_ref = refs[-2:]
    step = pl.program_id(0)
    odd = is_odd()

    @pl.when(jnp.logical_not(odd) if late else odd)
    def _():
        gathered = own_sum(
            step, send_ref, recv_ref, nodes_ref, ws_ref, wr_ref, table_ref, out_ref.shape[0]
        )
        ahead = dot(edges_ref[...], first_ref[0, 0]) + bias_ref[layer : layer + 1, :]
        out_ref[...] = ahead + gathered

    if late:

        @pl.when(odd)
        def _():
            out_ref[...] = refs[3][...]


def edge_kernel(
    rows,
    layer,
    size,
    valid_ref,
    owner_ref,
    send_ref,
    recv_ref,
    edges_ref,
    pre_ref,
    own_ref,
    prev_ref,
    next_ref,
    far_ref,
    ws_ref,
    wr_ref,
    wo_ref,
    gain_ref,
    shift_ref,
    out_ref,
    to_prev_ref,
    kept_ref,
    to_next_ref,
    table_ref,
    total_ref,
):
    step = pl.program_id(0)

    @pl.when(step == 0)
    def _():
        weight_s = ws_ref[0, 0]
        weight_r = wr_ref[0, 0]
        before = prev_ref[...]
        after = next_ref[...]
        table_ref[0 * rows : 1 * rows, :] = dot(before, weight_s).astype(BF16)
        table_ref[1 * rows : 2 * rows, :] = dot(after, weight_s).astype(BF16)
        table_ref[2 * rows : 3 * rows, :] = dot(before, weight_r).astype(BF16)
        table_ref[3 * rows : 4 * rows, :] = dot(after, weight_r).astype(BF16)
        away = owner_ref[layer] - lax.axis_index("patch")
        away = jnp.where(away < 0, away + size, away)
        hub = own_ref[:HUB, :]
        if size > 3:
            spot = jnp.clip(away - 2, 0, size - 4)
            hub = jnp.where(away > 1, far_ref[pl.ds(pl.multiple_of(spot * HUB, HUB), HUB), :], hub)
        hub = jnp.where(away == size - 1, prev_ref[:HUB, :], hub)
        hub = jnp.where(away == 1, next_ref[:HUB, :], hub)
        hub = jnp.where(away == 0, own_ref[:HUB, :], hub)
        table_ref[4 * rows : 4 * rows + HUB, :] = dot(hub, weight_s).astype(BF16)
        table_ref[4 * rows + HUB :, :] = jnp.zeros_like(table_ref[4 * rows + HUB :, :])
        total_ref[...] = jnp.zeros_like(total_ref)

    block = out_ref.shape[0]
    count = block // LANES
    spans = [
        tuple((start + at, 2 * LANES) for at in range(0, rows, 2 * LANES)) for start in (0, 2 * rows)
    ]
    hubs = ((3 * rows, LANES),)
    picks = jnp.concatenate(
        [
            selector(send_ref, step * count, count, spans[0] + spans[1]),
            selector(recv_ref, step * count, count, spans[0] + spans[1]),
            selector(send_ref, step * count, count, hubs),
        ],
        axis=1,
    )
    activated = silu(pre_ref[...] + dot(picks, table_ref[...])).astype(BF16)
    mixed = dot(activated, wo_ref[0])
    normed = layer_norm(mixed, gain_ref[layer : layer + 1, :], shift_ref[layer : layer + 1, :])
    spot = step * block + lax.broadcasted_iota(jnp.int32, (block, 1), 0)
    updated = jnp.where(spot < valid_ref[0], edges_ref[...].astype(F32) + normed, 0.0).astype(BF16)
    out_ref[...] = updated
    total_ref[...] += dot(selector_rows(recv_ref, step * count, count, 3 * rows), updated)

    @pl.when(step == pl.num_programs(0) - 1)
    def _():
        to_prev_ref[...] = total_ref[:rows, :].astype(BF16)
        kept_ref[...] = total_ref[rows : 2 * rows, :]
        to_next_ref[...] = total_ref[2 * rows :, :].astype(BF16)


def node_kernel(
    layer,
    nodes_ref,
    kept_ref,
    from_prev_ref,
    from_next_ref,
    wh_ref,
    wa_ref,
    bias_ref,
    wo_ref,
    gain_ref,
    shift_ref,
    *refs,
):
    out_ref = refs[-1]
    nodes = nodes_ref[...]
    summed = from_prev_ref[...].astype(F32) + kept_ref[...] + from_next_ref[...].astype(F32)
    pre_node = dot(nodes, wh_ref[0, 0]) + dot(summed.astype(BF16), wa_ref[0, 0])
    pre_node = pre_node + bias_ref[layer : layer + 1, :]
    mixed = dot(silu(pre_node).astype(BF16), wo_ref[0])
    normed = layer_norm(mixed, gain_ref[layer : layer + 1, :], shift_ref[layer : layer + 1, :])
    out_ref[...] = (nodes.astype(F32) + normed).astype(BF16)


def whole(shape):
    return pl.BlockSpec(shape, lambda *_: (0,) * len(shape))


def picked(shape, spot):
    block = (1,) * len(spot) + shape[len(spot) :]
    index = tuple(spot) + (0,) * (len(shape) - len(spot))
    return pl.BlockSpec(block, lambda *_: index)


def scalars():
    return pl.BlockSpec(memory_space=pltpu.SMEM)


def cost(flops, moved):
    return pl.CostEstimate(flops=flops, bytes_accessed=moved, transcendentals=0)


def local(
    nodes,
    edges,
    senders,
    receivers,
    valid_counts,
    hub_owner,
    edge_in,
    edge_bias,
    edge_out,
    edge_gain,
    edge_shift,
    node_in,
    node_bias,
    node_out,
    node_gain,
    node_shift,
):
    rows, width = nodes.shape
    slots = edges.shape[0]
    size = lax.axis_size("patch")
    block = min(512, slots)
    steps = slots // block
    send = senders.reshape(slots // LANES, LANES)
    recv = receivers.reshape(slots // LANES, LANES)
    by_block = pl.BlockSpec((block, width), lambda i: (i, 0))
    square = 2 * slots * width * width
    def start_edges(early):
        late = early is not None

        def active(i):
            return jnp.where(is_odd(), 0, i) if late else jnp.where(is_odd(), i, 0)

        def passive(i):
            return jnp.where(is_odd(), i, 0)

        given = (early,) if late else ()
        return pl.pallas_call(
            functools.partial(first_kernel, late, 0),
            out_shape=jax.ShapeDtypeStruct((slots, width), F32),
            grid=(steps,),
            in_specs=[whole(send.shape), whole(recv.shape), whole(nodes.shape)]
            + [picked(edge_in.shape, (0, 1)), picked(edge_in.shape, (0, 2))]
            + [pl.BlockSpec((block, width), lambda i: (active(i), 0))]
            + [picked(edge_in.shape, (0, 0)), whole(edge_bias.shape)]
            + [pl.BlockSpec((block, width), lambda i: (passive(i), 0))] * len(given),
            out_specs=pl.BlockSpec((block, width), lambda i: (i if late else active(i), 0)),
            scratch_shapes=[pltpu.VMEM((2 * rows, width), BF16)],
            compiler_params=pltpu.CompilerParams(vmem_limit_bytes=GRANT if late else None),
            cost_estimate=cost(2 * square, 6 * slots * width),
            name="late_part" if late else "early_part",
        )(send, recv, nodes, edge_in, edge_in, edges, edge_in, edge_bias, *given)

    early = start_edges(None)
    nodes, early = lax.optimization_barrier((nodes, early))
    for layer in range(LAYERS):
        from_prev = from_behind(nodes, "patch", 1)
        from_next = from_behind(nodes, "patch", -1)
        top = nodes[:HUB]
        far = [from_behind(top, "patch", -d) for d in range(2, size - 1)]
        far = jnp.concatenate(far, axis=0) if len(far) > 1 else (far[0] if far else top)
        ws = picked(edge_in.shape, (layer, 1))
        wr = picked(edge_in.shape, (layer, 2))
        if layer == 0:
            pre = start_edges(early)
        else:
            pre = pl.pallas_call(
                own_kernel,
                out_shape=jax.ShapeDtypeStruct((slots, width), F32),
                grid=(steps,),
                in_specs=[whole(send.shape), whole(recv.shape), whole(nodes.shape), ws, wr]
                + [by_block],
                out_specs=by_block,
                scratch_shapes=[pltpu.VMEM((2 * rows, width), BF16)],
                compiler_params=pltpu.CompilerParams(vmem_limit_bytes=GRANT),
                cost_estimate=cost(square, 8 * slots * width),
                name="own_part",
            )(send, recv, nodes, edge_in, edge_in, pre)
        edges, to_prev, kept, to_next = pl.pallas_call(
            functools.partial(edge_kernel, rows, layer, size),
            out_shape=(
                jax.ShapeDtypeStruct((slots, width), BF16),
                jax.ShapeDtypeStruct((rows, width), BF16),
                jax.ShapeDtypeStruct((rows, width), F32),
                jax.ShapeDtypeStruct((rows, width), BF16),
            ),
            grid=(steps,),
            in_specs=[
                scalars(),
                scalars(),
                whole(send.shape),
                whole(recv.shape),
                by_block,
                by_block,
                whole(nodes.shape),
                whole(nodes.shape),
                whole(nodes.shape),
                whole(far.shape),
                ws,
                wr,
                picked(edge_out.shape, (layer,)),
                whole(edge_gain.shape),
                whole(edge_shift.shape),
            ],
            out_specs=(by_block,) + (whole((rows, width)),) * 3,
            scratch_shapes=[
                pltpu.VMEM((4 * rows + LANES, width), BF16),
                pltpu.VMEM((3 * rows, width), F32),
            ],
            compiler_params=pltpu.CompilerParams(vmem_limit_bytes=GRANT),
            cost_estimate=cost(6 * square, 8 * slots * width),
            name="edge_part",
        )(
            valid_counts,
            hub_owner.reshape(-1),
            send,
            recv,
            edges,
            pre,
            nodes,
            from_prev,
            from_next,
            far,
            edge_in,
            edge_in,
            edge_out,
            edge_gain,
            edge_shift,
        )
        sum_next = from_behind(to_prev, "patch", -1)
        sum_prev = from_behind(to_next, "patch", 1)
        after = ()
        if layer + 1 < LAYERS:
            pre = pl.pallas_call(
                functools.partial(linear_kernel, layer + 1),
                out_shape=jax.ShapeDtypeStruct((slots, width), F32),
                grid=(steps,),
                in_specs=[
                    by_block,
                    picked(edge_in.shape, (layer + 1, 0)),
                    whole(edge_bias.shape),
                ],
                out_specs=by_block,
                compiler_params=pltpu.CompilerParams(vmem_limit_bytes=GRANT),
                cost_estimate=cost(square, 6 * slots * width),
                name="linear_part",
            )(edges, edge_in, edge_bias)
            after = (pre,)
        nodes = pl.pallas_call(
            functools.partial(node_kernel, layer),
            out_shape=jax.ShapeDtypeStruct((rows, width), BF16),
            grid=(1,),
            in_specs=[whole((rows, width))] * 4
            + [
                picked(node_in.shape, (layer, 0)),
                picked(node_in.shape, (layer, 1)),
                whole(node_bias.shape),
                picked(node_out.shape, (layer,)),
                whole(node_gain.shape),
                whole(node_shift.shape),
            ]
            + [pl.BlockSpec(memory_space=pl.ANY)] * len(after),
            out_specs=whole((rows, width)),
            compiler_params=pltpu.CompilerParams(vmem_limit_bytes=GRANT),
            cost_estimate=cost(6 * rows * width * width, 2 * width * width * 3),
            name="node_part",
        )(
            nodes,
            kept,
            sum_prev,
            sum_next,
            node_in,
            node_in,
            node_bias,
            node_out,
            node_gain,
            node_shift,
            *after,
        )
    return (nodes, edges)


def solution(mesh):
    placed = (
        P(("region", "patch"), None),
        P(("region", "patch"), None),
        P(("region", "patch")),
        P(("region", "patch")),
        P(("region", "patch")),
        P(None, "region"),
    ) + (P(),) * 10
    return jax.shard_map(
        local,
        mesh=mesh,
        in_specs=placed,
        out_specs=(P(("region", "patch"), None), P(("region", "patch"), None)),
        check_vma=False,
    )
```

```python
import functools

import jax
import jax.numpy as jnp
from jax import lax
from jax.experimental import pallas as pl
from jax.experimental.pallas import tpu as pltpu
from jax.sharding import PartitionSpec as P


HUB = 32
LAYERS = 2
LANES = 128
GRANT = 24 << 20

epsilon = 1e-05

F32 = jnp.float32
BF16 = jnp.bfloat16


def from_behind(block, axis, distance):
    size = lax.axis_size(axis)
    return lax.ppermute(block, axis, [((i - distance) % size, i) for i in range(size)])


def from_behind_by_parity(block, distance, parity):
    regions = range(parity, lax.axis_size("region"), 2)
    size = lax.axis_size("patch")
    route = [
        (r * size + (i - distance) % size, r * size + i) for r in regions for i in range(size)
    ]
    return lax.ppermute(block, ("region", "patch"), route)


def dot(left, right):
    return jnp.dot(left, right, preferred_element_type=F32)


def silu(value):
    half = value * 0.5
    return half + half * jnp.tanh(half)


def layer_norm(value, gain, shift):
    center = value - jnp.mean(value, axis=-1, keepdims=True)
    spread = jnp.mean(center * center, axis=-1, keepdims=True)
    return center * lax.rsqrt(spread + epsilon) * gain + shift


def selector(codes_ref, first, count, starts):
    groups = []
    for i in range(count):
        row = codes_ref[pl.ds(first + i, 1), :]
        parts = []
        for start, width in starts:
            near = jnp.clip(row - start, -1, width).astype(F32)
            near = jnp.broadcast_to(near, (LANES, LANES)).T.astype(BF16)
            for t in range(width // LANES):
                lane = lax.broadcasted_iota(jnp.int32, (LANES, LANES), 1) + t * LANES
                parts.append(jnp.where(near == lane.astype(BF16), BF16(1), BF16(0)))
        groups.append(jnp.concatenate(parts, axis=1))
    return jnp.concatenate(groups, axis=0)


def selector_rows(codes_ref, first, count, width):
    tile = 2 * LANES
    groups = []
    for i in range(count):
        row = codes_ref[pl.ds(first + i, 1), :]
        parts = []
        for start in range(0, width, tile):
            near = jnp.clip(row - start, -1, tile).astype(F32)
            near = jnp.broadcast_to(near, (tile, LANES)).astype(BF16)
            sub = lax.broadcasted_iota(jnp.int32, (tile, LANES), 0).astype(BF16)
            parts.append(jnp.where(near == sub, BF16(1), BF16(0)))
        groups.append(jnp.concatenate(parts, axis=0))
    return jnp.concatenate(groups, axis=1)


def linear_kernel(layer, edges_ref, weight_ref, bias_ref, out_ref):
    out_ref[...] = dot(edges_ref[...], weight_ref[0, 0]) + bias_ref[layer : layer + 1, :]


def own_table(nodes, ws_ref, wr_ref, table_ref):
    rows = nodes.shape[0]
    table_ref[:rows, :] = dot(nodes, ws_ref[0, 0]).astype(BF16)
    table_ref[rows:, :] = dot(nodes, wr_ref[0, 0]).astype(BF16)


def own_picks(send_ref, recv_ref, first, count, rows):
    spans = tuple((rows + at, 2 * LANES) for at in range(0, rows, 2 * LANES))
    return jnp.concatenate(
        [selector(send_ref, first, count, spans), selector(recv_ref, first, count, spans)],
        axis=1,
    )


def own_sum(step, send_ref, recv_ref, nodes_ref, ws_ref, wr_ref, table_ref, edges):
    rows = nodes_ref.shape[0]

    @pl.when(step == 0)
    def _():
        own_table(nodes_ref[...], ws_ref, wr_ref, table_ref)

    count = edges // LANES
    return dot(own_picks(send_ref, recv_ref, step * count, count, rows), table_ref[...])


def own_kernel(send_ref, recv_ref, nodes_ref, ws_ref, wr_ref, pre_ref, out_ref, table_ref):
    gathered = own_sum(
        pl.program_id(0), send_ref, recv_ref, nodes_ref, ws_ref, wr_ref, table_ref, out_ref.shape[0]
    )
    out_ref[...] = pre_ref[...] + gathered


def is_odd():
    return lax.axis_index("region") % 2 == 1


def first_kernel(layer, send_ref, recv_ref, nodes_ref, ws_ref, wr_ref, *refs):
    edges_ref, first_ref, bias_ref, out_ref, table_ref = refs
    gathered = own_sum(
        pl.program_id(0), send_ref, recv_ref, nodes_ref, ws_ref, wr_ref, table_ref, out_ref.shape[0]
    )
    ahead = dot(edges_ref[...], first_ref[0, 0]) + bias_ref[layer : layer + 1, :]
    out_ref[...] = ahead + gathered


def is_odd():
    return lax.axis_index("region") % 2 == 1


def edge_kernel(rows, layer, size, *refs):
    valid_ref, owner_ref, send_ref, recv_ref, edges_ref, pre_ref, own_ref = refs[:7]
    near = refs[7:-13]
    far_ref, ws_ref, wr_ref, wo_ref, gain_ref, shift_ref = refs[-13:-7]
    out_ref, to_prev_ref, kept_ref, to_next_ref = refs[-7:-3]
    near_ref, table_ref, total_ref = refs[-3:]
    step = pl.program_id(0)

    @pl.when(step == 0)
    def _():
        odd = is_odd()
        for side in range(2):
            block = near[side][...]
            if len(near) > 2:
                block = jnp.where(odd, near[side + 2][...], block)
            near_ref[side * rows : (side + 1) * rows, :] = block
        blocks = near_ref[...]
        weight_s = ws_ref[0, 0]
        table_ref[: 2 * rows, :] = dot(blocks, weight_s).astype(BF16)
        table_ref[2 * rows : 4 * rows, :] = dot(blocks, wr_ref[0, 0]).astype(BF16)
        away = owner_ref[layer] - lax.axis_index("patch")
        away = jnp.where(away < 0, away + size, away)
        hub = own_ref[:HUB, :]
        if size > 3:
            spot = jnp.clip(away - 2, 0, size - 4)
            hub = jnp.where(away > 1, far_ref[pl.ds(pl.multiple_of(spot * HUB, HUB), HUB), :], hub)
        hub = jnp.where(away == size - 1, near_ref[:HUB, :], hub)
        hub = jnp.where(away == 1, near_ref[rows : rows + HUB, :], hub)
        hub = jnp.where(away == 0, own_ref[:HUB, :], hub)
        table_ref[4 * rows : 4 * rows + HUB, :] = dot(hub, weight_s).astype(BF16)
        table_ref[4 * rows + HUB :, :] = jnp.zeros_like(table_ref[4 * rows + HUB :, :])
        total_ref[...] = jnp.zeros_like(total_ref)

    block = out_ref.shape[0]
    count = block // LANES
    spans = [
        tuple((start + at, 2 * LANES) for at in range(0, rows, 2 * LANES)) for start in (0, 2 * rows)
    ]
    hubs = ((3 * rows, LANES),)
    picks = jnp.concatenate(
        [
            selector(send_ref, step * count, count, spans[0] + spans[1]),
            selector(recv_ref, step * count, count, spans[0] + spans[1]),
            selector(send_ref, step * count, count, hubs),
        ],
        axis=1,
    )
    activated = silu(pre_ref[...] + dot(picks, table_ref[...])).astype(BF16)
    mixed = dot(activated, wo_ref[0])
    normed = layer_norm(mixed, gain_ref[layer : layer + 1, :], shift_ref[layer : layer + 1, :])
    spot = step * block + lax.broadcasted_iota(jnp.int32, (block, 1), 0)
    updated = jnp.where(spot < valid_ref[0], edges_ref[...].astype(F32) + normed, 0.0).astype(BF16)
    out_ref[...] = updated
    total_ref[...] += dot(selector_rows(recv_ref, step * count, count, 3 * rows), updated)

    @pl.when(step == pl.num_programs(0) - 1)
    def _():
        to_prev_ref[...] = total_ref[:rows, :].astype(BF16)
        kept_ref[...] = total_ref[rows : 2 * rows, :]
        to_next_ref[...] = total_ref[2 * rows :, :].astype(BF16)


def node_kernel(
    layer,
    nodes_ref,
    kept_ref,
    from_prev_ref,
    from_next_ref,
    wh_ref,
    wa_ref,
    bias_ref,
    wo_ref,
    gain_ref,
    shift_ref,
    *refs,
):
    out_ref = refs[-1]
    nodes = nodes_ref[...]
    summed = from_prev_ref[...].astype(F32) + kept_ref[...] + from_next_ref[...].astype(F32)
    pre_node = dot(nodes, wh_ref[0, 0]) + dot(summed.astype(BF16), wa_ref[0, 0])
    pre_node = pre_node + bias_ref[layer : layer + 1, :]
    mixed = dot(silu(pre_node).astype(BF16), wo_ref[0])
    normed = layer_norm(mixed, gain_ref[layer : layer + 1, :], shift_ref[layer : layer + 1, :])
    out_ref[...] = (nodes.astype(F32) + normed).astype(BF16)


def whole(shape):
    return pl.BlockSpec(shape, lambda *_: (0,) * len(shape))


def picked(shape, spot):
    block = (1,) * len(spot) + shape[len(spot) :]
    index = tuple(spot) + (0,) * (len(shape) - len(spot))
    return pl.BlockSpec(block, lambda *_: index)


def scalars():
    return pl.BlockSpec(memory_space=pltpu.SMEM)


def cost(flops, moved):
    return pl.CostEstimate(flops=flops, bytes_accessed=moved, transcendentals=0)


def local(
    nodes,
    edges,
    senders,
    receivers,
    valid_counts,
    hub_owner,
    edge_in,
    edge_bias,
    edge_out,
    edge_gain,
    edge_shift,
    node_in,
    node_bias,
    node_out,
    node_gain,
    node_shift,
):
    rows, width = nodes.shape
    slots = edges.shape[0]
    size = lax.axis_size("patch")
    block = min(512, slots)
    steps = slots // block
    send = senders.reshape(slots // LANES, LANES)
    recv = receivers.reshape(slots // LANES, LANES)
    by_block = pl.BlockSpec((block, width), lambda i: (i, 0))
    square = 2 * slots * width * width

    def start_edges():
        return pl.pallas_call(
            functools.partial(first_kernel, 0),
            out_shape=jax.ShapeDtypeStruct((slots, width), F32),
            grid=(steps,),
            in_specs=[whole(send.shape), whole(recv.shape), whole(nodes.shape)]
            + [picked(edge_in.shape, (0, 1)), picked(edge_in.shape, (0, 2)), by_block]
            + [picked(edge_in.shape, (0, 0)), whole(edge_bias.shape)],
            out_specs=by_block,
            scratch_shapes=[pltpu.VMEM((2 * rows, width), BF16)],
            compiler_params=pltpu.CompilerParams(vmem_limit_bytes=GRANT),
            cost_estimate=cost(2 * square, 6 * slots * width),
            name="first_part",
        )(send, recv, nodes, edge_in, edge_in, edges, edge_in, edge_bias)

    for layer in range(LAYERS):
        if layer == 0:
            near = [from_behind_by_parity(nodes, d, 0) for d in (1, -1)]
        else:
            near = [from_behind(nodes, "patch", d) for d in (1, -1)]
        top = nodes[:HUB]
        far = [from_behind(top, "patch", -d) for d in range(2, size - 1)]
        far = jnp.concatenate(far, axis=0) if len(far) > 1 else (far[0] if far else top)
        ws = picked(edge_in.shape, (layer, 1))
        wr = picked(edge_in.shape, (layer, 2))
        if layer == 0:
            pre = start_edges()
            nodes, pre = lax.optimization_barrier((nodes, pre))
            near += [from_behind_by_parity(nodes, d, 1) for d in (1, -1)]
        else:
            pre = pl.pallas_call(
                own_kernel,
                out_shape=jax.ShapeDtypeStruct((slots, width), F32),
                grid=(steps,),
                in_specs=[whole(send.shape), whole(recv.shape), whole(nodes.shape), ws, wr]
                + [by_block],
                out_specs=by_block,
                scratch_shapes=[pltpu.VMEM((2 * rows, width), BF16)],
                compiler_params=pltpu.CompilerParams(vmem_limit_bytes=GRANT),
                cost_estimate=cost(square, 8 * slots * width),
                name="own_part",
            )(send, recv, nodes, edge_in, edge_in, pre)
        edges, to_prev, kept, to_next = pl.pallas_call(
            functools.partial(edge_kernel, rows, layer, size),
            out_shape=(
                jax.ShapeDtypeStruct((slots, width), BF16),
                jax.ShapeDtypeStruct((rows, width), BF16),
                jax.ShapeDtypeStruct((rows, width), F32),
                jax.ShapeDtypeStruct((rows, width), BF16),
            ),
            grid=(steps,),
            in_specs=[
                scalars(),
                scalars(),
                whole(send.shape),
                whole(recv.shape),
                by_block,
                by_block,
            ]
            + [whole(nodes.shape)] * (1 + len(near))
            + [
                whole(far.shape),
                ws,
                wr,
                picked(edge_out.shape, (layer,)),
                whole(edge_gain.shape),
                whole(edge_shift.shape),
            ],
            out_specs=(by_block,) + (whole((rows, width)),) * 3,
            scratch_shapes=[
                pltpu.VMEM((2 * rows, width), BF16),
                pltpu.VMEM((4 * rows + LANES, width), BF16),
                pltpu.VMEM((3 * rows, width), F32),
            ],
            compiler_params=pltpu.CompilerParams(vmem_limit_bytes=GRANT),
            cost_estimate=cost(6 * square, 8 * slots * width),
            name="edge_part",
        )(
            valid_counts,
            hub_owner.reshape(-1),
            send,
            recv,
            edges,
            pre,
            nodes,
            *near,
            far,
            edge_in,
            edge_in,
            edge_out,
            edge_gain,
            edge_shift,
        )
        sum_next = from_behind(to_prev, "patch", -1)
        sum_prev = from_behind(to_next, "patch", 1)
        after = ()
        if layer + 1 < LAYERS:
            pre = pl.pallas_call(
                functools.partial(linear_kernel, layer + 1),
                out_shape=jax.ShapeDtypeStruct((slots, width), F32),
                grid=(steps,),
                in_specs=[
                    by_block,
                    picked(edge_in.shape, (layer + 1, 0)),
                    whole(edge_bias.shape),
                ],
                out_specs=by_block,
                compiler_params=pltpu.CompilerParams(vmem_limit_bytes=GRANT),
                cost_estimate=cost(square, 6 * slots * width),
                name="linear_part",
            )(edges, edge_in, edge_bias)
            after = (pre,)
        nodes = pl.pallas_call(
            functools.partial(node_kernel, layer),
            out_shape=jax.ShapeDtypeStruct((rows, width), BF16),
            grid=(1,),
            in_specs=[whole((rows, width))] * 4
            + [
                picked(node_in.shape, (layer, 0)),
                picked(node_in.shape, (layer, 1)),
                whole(node_bias.shape),
                picked(node_out.shape, (layer,)),
                whole(node_gain.shape),
                whole(node_shift.shape),
            ]
            + [pl.BlockSpec(memory_space=pl.ANY)] * len(after),
            out_specs=whole((rows, width)),
            compiler_params=pltpu.CompilerParams(vmem_limit_bytes=GRANT),
            cost_estimate=cost(6 * rows * width * width, 2 * width * width * 3),
            name="node_part",
        )(
            nodes,
            kept,
            sum_prev,
            sum_next,
            node_in,
            node_in,
            node_bias,
            node_out,
            node_gain,
            node_shift,
            *after,
        )
    return (nodes, edges)


def solution(mesh):
    placed = (
        P(("region", "patch"), None),
        P(("region", "patch"), None),
        P(("region", "patch")),
        P(("region", "patch")),
        P(("region", "patch")),
        P(None, "region"),
    ) + (P(),) * 10
    return jax.shard_map(
        local,
        mesh=mesh,
        in_specs=placed,
        out_specs=(P(("region", "patch"), None), P(("region", "patch"), None)),
        check_vma=False,
    )
```

```python
import functools

import jax
import jax.numpy as jnp
from jax import lax
from jax.experimental import pallas as pl
from jax.experimental.pallas import tpu as pltpu
from jax.sharding import PartitionSpec as P


HUB = 32
LAYERS = 2
LANES = 128
GRANT = 24 << 20

epsilon = 1e-05

F32 = jnp.float32
BF16 = jnp.bfloat16


def from_behind(block, axis, distance):
    size = lax.axis_size(axis)
    return lax.ppermute(block, axis, [((i - distance) % size, i) for i in range(size)])


def dot(left, right):
    return jnp.dot(left, right, preferred_element_type=F32)


def silu(value):
    half = value * 0.5
    return half + half * jnp.tanh(half)


def layer_norm(value, gain, shift):
    center = value - jnp.mean(value, axis=-1, keepdims=True)
    spread = jnp.mean(center * center, axis=-1, keepdims=True)
    return center * lax.rsqrt(spread + epsilon) * gain + shift


def selector(codes_ref, first, count, starts):
    groups = []
    for i in range(count):
        row = codes_ref[pl.ds(first + i, 1), :]
        parts = []
        for start, width in starts:
            near = jnp.clip(row - start, -1, width).astype(F32)
            near = jnp.broadcast_to(near, (LANES, LANES)).T.astype(BF16)
            for t in range(width // LANES):
                lane = lax.broadcasted_iota(jnp.int32, (LANES, LANES), 1) + t * LANES
                parts.append(jnp.where(near == lane.astype(BF16), BF16(1), BF16(0)))
        groups.append(jnp.concatenate(parts, axis=1))
    return jnp.concatenate(groups, axis=0)


def selector_rows(codes_ref, first, count, width):
    tile = 2 * LANES
    groups = []
    for i in range(count):
        row = codes_ref[pl.ds(first + i, 1), :]
        parts = []
        for start in range(0, width, tile):
            near = jnp.clip(row - start, -1, tile).astype(F32)
            near = jnp.broadcast_to(near, (tile, LANES)).astype(BF16)
            sub = lax.broadcasted_iota(jnp.int32, (tile, LANES), 0).astype(BF16)
            parts.append(jnp.where(near == sub, BF16(1), BF16(0)))
        groups.append(jnp.concatenate(parts, axis=0))
    return jnp.concatenate(groups, axis=1)


def linear_kernel(layer, edges_ref, weight_ref, bias_ref, out_ref):
    out_ref[...] = dot(edges_ref[...], weight_ref[0, 0]) + bias_ref[layer : layer + 1, :]


def own_table(nodes, ws_ref, wr_ref, table_ref):
    rows = nodes.shape[0]
    table_ref[:rows, :] = dot(nodes, ws_ref[0, 0]).astype(BF16)
    table_ref[rows:, :] = dot(nodes, wr_ref[0, 0]).astype(BF16)


def own_picks(send_ref, recv_ref, first, count, rows):
    spans = tuple((rows + at, 2 * LANES) for at in range(0, rows, 2 * LANES))
    return jnp.concatenate(
        [selector(send_ref, first, count, spans), selector(recv_ref, first, count, spans)],
        axis=1,
    )


def own_sum(step, send_ref, recv_ref, nodes_ref, ws_ref, wr_ref, table_ref, edges):
    rows = nodes_ref.shape[0]

    @pl.when(step == 0)
    def _():
        own_table(nodes_ref[...], ws_ref, wr_ref, table_ref)

    count = edges // LANES
    return dot(own_picks(send_ref, recv_ref, step * count, count, rows), table_ref[...])


def own_kernel(send_ref, recv_ref, nodes_ref, ws_ref, wr_ref, pre_ref, out_ref, table_ref):
    gathered = own_sum(
        pl.program_id(0), send_ref, recv_ref, nodes_ref, ws_ref, wr_ref, table_ref, out_ref.shape[0]
    )
    out_ref[...] = pre_ref[...] + gathered


def first_kernel(late, layer, steps, *refs):
    send_ref, recv_ref, nodes_ref, bias_ref, edges_ref, weights_ref = refs[:6]
    out_ref, table_ref, weight_buf, edges_buf, out_buf, weight_sem, in_sem, out_sem = refs[-8:]
    rows = nodes_ref.shape[0]
    block = edges_buf.shape[0] // steps
    count = block // LANES

    def span(i):
        return pl.ds(i * block, block)

    def fetch(i):
        return pltpu.make_async_copy(edges_ref.at[span(i)], edges_buf.at[span(i)], in_sem.at[i])

    def weight(i):
        return pltpu.make_async_copy(weights_ref.at[layer, i], weight_buf.at[i], weight_sem.at[i])

    def put(i):
        return pltpu.make_async_copy(out_buf.at[span(i)], out_ref.at[span(i)], out_sem.at[i])

    def work(span_of):
        for i in (1, 2, 0):
            weight(i).start()
        for i in span_of:
            fetch(i).start()
        weight(1).wait()
        table_ref[:rows, :] = dot(nodes_ref[...], weight_buf[1]).astype(BF16)
        weight(2).wait()
        table_ref[rows:, :] = dot(nodes_ref[...], weight_buf[2]).astype(BF16)
        weight(0).wait()
        for i in span_of:
            fetch(i).wait()
            picks = own_picks(send_ref, recv_ref, i * count, count, rows)
            total = dot(picks, table_ref[...]) + dot(edges_buf[span(i), :], weight_buf[0])
            out_buf[span(i), :] = total + bias_ref[layer : layer + 1, :]
            put(i).start()
        for i in span_of:
            put(i).wait()

    even = lax.axis_index("region") % 2 == 0
    early = steps // 2

    @pl.when(even)
    def _():
        work(range(early, steps) if late else range(early))

    if late:

        @pl.when(jnp.logical_not(even))
        def _():
            work(range(steps))


def edge_kernel(rows, layer, size, *refs):
    valid_ref, owner_ref, send_ref, recv_ref, edges_ref, pre_ref, own_ref = refs[:7]
    near = refs[7:-13]
    far_ref, ws_ref, wr_ref, wo_ref, gain_ref, shift_ref = refs[-13:-7]
    out_ref, to_prev_ref, kept_ref, to_next_ref = refs[-7:-3]
    near_ref, table_ref, total_ref = refs[-3:]
    step = pl.program_id(0)

    @pl.when(step == 0)
    def _():
        for side in range(2):
            near_ref[side * rows : (side + 1) * rows, :] = near[side][...]
        blocks = near_ref[...]
        weight_s = ws_ref[0, 0]
        table_ref[: 2 * rows, :] = dot(blocks, weight_s).astype(BF16)
        table_ref[2 * rows : 4 * rows, :] = dot(blocks, wr_ref[0, 0]).astype(BF16)
        away = owner_ref[layer] - lax.axis_index("patch")
        away = jnp.where(away < 0, away + size, away)
        hub = own_ref[:HUB, :]
        if size > 3:
            spot = jnp.clip(away - 2, 0, size - 4)
            hub = jnp.where(away > 1, far_ref[pl.ds(pl.multiple_of(spot * HUB, HUB), HUB), :], hub)
        hub = jnp.where(away == size - 1, near_ref[:HUB, :], hub)
        hub = jnp.where(away == 1, near_ref[rows : rows + HUB, :], hub)
        hub = jnp.where(away == 0, own_ref[:HUB, :], hub)
        table_ref[4 * rows : 4 * rows + HUB, :] = dot(hub, weight_s).astype(BF16)
        table_ref[4 * rows + HUB :, :] = jnp.zeros_like(table_ref[4 * rows + HUB :, :])
        total_ref[...] = jnp.zeros_like(total_ref)

    block = out_ref.shape[0]
    count = block // LANES
    spans = [
        tuple((start + at, 2 * LANES) for at in range(0, rows, 2 * LANES)) for start in (0, 2 * rows)
    ]
    hubs = ((3 * rows, LANES),)
    picks = jnp.concatenate(
        [
            selector(send_ref, step * count, count, spans[0] + spans[1]),
            selector(recv_ref, step * count, count, spans[0] + spans[1]),
            selector(send_ref, step * count, count, hubs),
        ],
        axis=1,
    )
    activated = silu(pre_ref[...] + dot(picks, table_ref[...])).astype(BF16)
    mixed = dot(activated, wo_ref[0])
    normed = layer_norm(mixed, gain_ref[layer : layer + 1, :], shift_ref[layer : layer + 1, :])
    spot = step * block + lax.broadcasted_iota(jnp.int32, (block, 1), 0)
    updated = jnp.where(spot < valid_ref[0], edges_ref[...].astype(F32) + normed, 0.0).astype(BF16)
    out_ref[...] = updated
    total_ref[...] += dot(selector_rows(recv_ref, step * count, count, 3 * rows), updated)

    @pl.when(step == pl.num_programs(0) - 1)
    def _():
        to_prev_ref[...] = total_ref[:rows, :].astype(BF16)
        kept_ref[...] = total_ref[rows : 2 * rows, :]
        to_next_ref[...] = total_ref[2 * rows :, :].astype(BF16)


def node_kernel(
    layer,
    nodes_ref,
    kept_ref,
    from_prev_ref,
    from_next_ref,
    wh_ref,
    wa_ref,
    bias_ref,
    wo_ref,
    gain_ref,
    shift_ref,
    *refs,
):
    out_ref = refs[-1]
    nodes = nodes_ref[...]
    summed = from_prev_ref[...].astype(F32) + kept_ref[...] + from_next_ref[...].astype(F32)
    pre_node = dot(nodes, wh_ref[0, 0]) + dot(summed.astype(BF16), wa_ref[0, 0])
    pre_node = pre_node + bias_ref[layer : layer + 1, :]
    mixed = dot(silu(pre_node).astype(BF16), wo_ref[0])
    normed = layer_norm(mixed, gain_ref[layer : layer + 1, :], shift_ref[layer : layer + 1, :])
    out_ref[...] = (nodes.astype(F32) + normed).astype(BF16)


def whole(shape):
    return pl.BlockSpec(shape, lambda *_: (0,) * len(shape))


def picked(shape, spot):
    block = (1,) * len(spot) + shape[len(spot) :]
    index = tuple(spot) + (0,) * (len(shape) - len(spot))
    return pl.BlockSpec(block, lambda *_: index)


def scalars():
    return pl.BlockSpec(memory_space=pltpu.SMEM)


def cost(flops, moved):
    return pl.CostEstimate(flops=flops, bytes_accessed=moved, transcendentals=0)


def local(
    nodes,
    edges,
    senders,
    receivers,
    valid_counts,
    hub_owner,
    edge_in,
    edge_bias,
    edge_out,
    edge_gain,
    edge_shift,
    node_in,
    node_bias,
    node_out,
    node_gain,
    node_shift,
):
    rows, width = nodes.shape
    slots = edges.shape[0]
    size = lax.axis_size("patch")
    block = min(512, slots)
    steps = slots // block
    send = senders.reshape(slots // LANES, LANES)
    recv = receivers.reshape(slots // LANES, LANES)
    by_block = pl.BlockSpec((block, width), lambda i: (i, 0))
    square = 2 * slots * width * width

    def start_edges(held):
        late = held is not None
        anywhere = pl.BlockSpec(memory_space=pl.ANY)
        given = (held,) if late else ()
        fixed = [
            pltpu.with_memory_space_constraint(value, pltpu.HBM)
            for value in (send, recv, nodes, edge_bias, edges, edge_in)
        ]
        return pl.pallas_call(
            functools.partial(first_kernel, late, 0, steps),
            out_shape=jax.ShapeDtypeStruct((slots, width), F32),
            in_specs=[whole(send.shape), whole(recv.shape), whole(nodes.shape)]
            + [whole(edge_bias.shape), anywhere, anywhere]
            + [anywhere] * len(given),
            out_specs=anywhere,
            grid=(1,),
            input_output_aliases={6: 0} if late else {},
            scratch_shapes=[
                pltpu.VMEM((2 * rows, width), BF16),
                pltpu.VMEM((3, width, width), BF16),
                pltpu.VMEM((slots, width), BF16),
                pltpu.VMEM((slots, width), F32),
                pltpu.SemaphoreType.DMA((3,)),
                pltpu.SemaphoreType.DMA((steps,)),
                pltpu.SemaphoreType.DMA((steps,)),
            ],
            compiler_params=pltpu.CompilerParams(vmem_limit_bytes=GRANT),
            cost_estimate=cost(2 * square, 6 * slots * width),
            name="late_part" if late else "early_part",
        )(*fixed, *given)

    early = start_edges(None)
    sent, early = lax.optimization_barrier((nodes, early))
    for layer in range(LAYERS):
        near = [from_behind(sent, "patch", d) for d in (1, -1)]
        top = sent[:HUB]
        far = [from_behind(top, "patch", -d) for d in range(2, size - 1)]
        far = jnp.concatenate(far, axis=0) if len(far) > 1 else (far[0] if far else top)
        ws = picked(edge_in.shape, (layer, 1))
        wr = picked(edge_in.shape, (layer, 2))
        if layer == 0:
            pre = start_edges(early)
        else:
            pre = pl.pallas_call(
                own_kernel,
                out_shape=jax.ShapeDtypeStruct((slots, width), F32),
                grid=(steps,),
                in_specs=[whole(send.shape), whole(recv.shape), whole(nodes.shape), ws, wr]
                + [by_block],
                out_specs=by_block,
                scratch_shapes=[pltpu.VMEM((2 * rows, width), BF16)],
                compiler_params=pltpu.CompilerParams(vmem_limit_bytes=GRANT),
                cost_estimate=cost(square, 8 * slots * width),
                name="own_part",
            )(send, recv, nodes, edge_in, edge_in, pre)
        edges, to_prev, kept, to_next = pl.pallas_call(
            functools.partial(edge_kernel, rows, layer, size),
            out_shape=(
                jax.ShapeDtypeStruct((slots, width), BF16),
                jax.ShapeDtypeStruct((rows, width), BF16),
                jax.ShapeDtypeStruct((rows, width), F32),
                jax.ShapeDtypeStruct((rows, width), BF16),
            ),
            grid=(steps,),
            in_specs=[
                scalars(),
                scalars(),
                whole(send.shape),
                whole(recv.shape),
                by_block,
                by_block,
            ]
            + [whole(nodes.shape)] * (1 + len(near))
            + [
                whole(far.shape),
                ws,
                wr,
                picked(edge_out.shape, (layer,)),
                whole(edge_gain.shape),
                whole(edge_shift.shape),
            ],
            out_specs=(by_block,) + (whole((rows, width)),) * 3,
            scratch_shapes=[
                pltpu.VMEM((2 * rows, width), BF16),
                pltpu.VMEM((4 * rows + LANES, width), BF16),
                pltpu.VMEM((3 * rows, width), F32),
            ],
            compiler_params=pltpu.CompilerParams(vmem_limit_bytes=GRANT),
            cost_estimate=cost(6 * square, 8 * slots * width),
            name="edge_part",
        )(
            valid_counts,
            hub_owner.reshape(-1),
            send,
            recv,
            edges,
            pre,
            nodes,
            *near,
            far,
            edge_in,
            edge_in,
            edge_out,
            edge_gain,
            edge_shift,
        )
        sum_next = from_behind(to_prev, "patch", -1)
        sum_prev = from_behind(to_next, "patch", 1)
        after = ()
        if layer + 1 < LAYERS:
            pre = pl.pallas_call(
                functools.partial(linear_kernel, layer + 1),
                out_shape=jax.ShapeDtypeStruct((slots, width), F32),
                grid=(steps,),
                in_specs=[
                    by_block,
                    picked(edge_in.shape, (layer + 1, 0)),
                    whole(edge_bias.shape),
                ],
                out_specs=by_block,
                compiler_params=pltpu.CompilerParams(vmem_limit_bytes=GRANT),
                cost_estimate=cost(square, 6 * slots * width),
                name="linear_part",
            )(edges, edge_in, edge_bias)
            after = (pre,)
        nodes = pl.pallas_call(
            functools.partial(node_kernel, layer),
            out_shape=jax.ShapeDtypeStruct((rows, width), BF16),
            grid=(1,),
            in_specs=[whole((rows, width))] * 4
            + [
                picked(node_in.shape, (layer, 0)),
                picked(node_in.shape, (layer, 1)),
                whole(node_bias.shape),
                picked(node_out.shape, (layer,)),
                whole(node_gain.shape),
                whole(node_shift.shape),
            ]
            + [pl.BlockSpec(memory_space=pl.ANY)] * len(after),
            out_specs=whole((rows, width)),
            compiler_params=pltpu.CompilerParams(vmem_limit_bytes=GRANT),
            cost_estimate=cost(6 * rows * width * width, 2 * width * width * 3),
            name="node_part",
        )(
            nodes,
            kept,
            sum_prev,
            sum_next,
            node_in,
            node_in,
            node_bias,
            node_out,
            node_gain,
            node_shift,
            *after,
        )
        sent = nodes
    return (nodes, edges)


def solution(mesh):
    placed = (
        P(("region", "patch"), None),
        P(("region", "patch"), None),
        P(("region", "patch")),
        P(("region", "patch")),
        P(("region", "patch")),
        P(None, "region"),
    ) + (P(),) * 10
    return jax.shard_map(
        local,
        mesh=mesh,
        in_specs=placed,
        out_specs=(P(("region", "patch"), None), P(("region", "patch"), None)),
        check_vma=False,
    )
```

```python
import functools

import jax
import jax.numpy as jnp
from jax import lax
from jax.experimental import pallas as pl
from jax.experimental.pallas import tpu as pltpu
from jax.sharding import PartitionSpec as P


HUB = 32
LAYERS = 2
LANES = 128
GRANT = 24 << 20

epsilon = 1e-05

F32 = jnp.float32
BF16 = jnp.bfloat16


def from_behind(block, axis, distance):
    size = lax.axis_size(axis)
    return lax.ppermute(block, axis, [((i - distance) % size, i) for i in range(size)])


def dot(left, right):
    return jnp.dot(left, right, preferred_element_type=F32)


def silu_of_half(half):
    return half + half * jnp.tanh(half)


def half_table(rows, weight):
    return (dot(rows, weight) * 0.5).astype(BF16)


def layer_norm(value, gain, shift):
    center = value - jnp.mean(value, axis=-1, keepdims=True)
    spread = jnp.mean(center * center, axis=-1, keepdims=True)
    return center * lax.rsqrt(spread + epsilon) * gain + shift


def selector(codes_ref, first, count, starts):
    groups = []
    for i in range(count):
        row = codes_ref[pl.ds(first + i, 1), :]
        parts = []
        for start, width in starts:
            near = jnp.clip(row - start, -1, width).astype(F32)
            near = jnp.broadcast_to(near, (LANES, LANES)).T.astype(BF16)
            for t in range(width // LANES):
                lane = lax.broadcasted_iota(jnp.int32, (LANES, LANES), 1) + t * LANES
                parts.append(jnp.where(near == lane.astype(BF16), BF16(1), BF16(0)))
        groups.append(jnp.concatenate(parts, axis=1))
    return jnp.concatenate(groups, axis=0)


def selector_rows(codes_ref, first, count, width, valid):
    tile = 2 * LANES
    groups = []
    for i in range(count):
        slot = (first + i) * LANES + lax.broadcasted_iota(jnp.int32, (1, LANES), 1)
        row = jnp.where(slot < valid, codes_ref[pl.ds(first + i, 1), :], -1)
        parts = []
        for start in range(0, width, tile):
            near = jnp.clip(row - start, -1, tile).astype(F32)
            near = jnp.broadcast_to(near, (tile, LANES)).astype(BF16)
            sub = lax.broadcasted_iota(jnp.int32, (tile, LANES), 0).astype(BF16)
            parts.append(jnp.where(near == sub, BF16(1), BF16(0)))
        groups.append(jnp.concatenate(parts, axis=0))
    return jnp.concatenate(groups, axis=1)


def linear_kernel(layer, edges_ref, weight_ref, bias_ref, out_ref):
    ahead = dot(edges_ref[...], weight_ref[0, 0]) + bias_ref[layer : layer + 1, :]
    out_ref[...] = ahead * 0.5


def own_table(nodes, ws_ref, wr_ref, table_ref):
    rows = nodes.shape[0]
    table_ref[:rows, :] = half_table(nodes, ws_ref[0, 0])
    table_ref[rows:, :] = half_table(nodes, wr_ref[0, 0])


def own_picks(send_ref, recv_ref, first, count, rows):
    spans = tuple((rows + at, 2 * LANES) for at in range(0, rows, 2 * LANES))
    return jnp.concatenate(
        [selector(send_ref, first, count, spans), selector(recv_ref, first, count, spans)],
        axis=1,
    )


def own_sum(step, send_ref, recv_ref, nodes_ref, ws_ref, wr_ref, table_ref, edges):
    rows = nodes_ref.shape[0]

    @pl.when(step == 0)
    def _():
        own_table(nodes_ref[...], ws_ref, wr_ref, table_ref)

    count = edges // LANES
    return dot(own_picks(send_ref, recv_ref, step * count, count, rows), table_ref[...])


def own_kernel(send_ref, recv_ref, nodes_ref, ws_ref, wr_ref, pre_ref, out_ref, table_ref):
    gathered = own_sum(
        pl.program_id(0), send_ref, recv_ref, nodes_ref, ws_ref, wr_ref, table_ref, out_ref.shape[0]
    )
    out_ref[...] = pre_ref[...] + gathered


def first_kernel(late, layer, steps, *refs):
    send_ref, recv_ref, nodes_ref, bias_ref, edges_ref, weights_ref = refs[:6]
    out_ref, table_ref, weight_buf, edges_buf, out_buf, weight_sem, in_sem, out_sem = refs[-8:]
    rows = nodes_ref.shape[0]
    block = edges_buf.shape[0] // steps
    count = block // LANES

    def span(i):
        return pl.ds(i * block, block)

    def fetch(i):
        return pltpu.make_async_copy(edges_ref.at[span(i)], edges_buf.at[span(i)], in_sem.at[i])

    def weight(i):
        return pltpu.make_async_copy(weights_ref.at[layer, i], weight_buf.at[i], weight_sem.at[i])

    def put(i):
        return pltpu.make_async_copy(out_buf.at[span(i)], out_ref.at[span(i)], out_sem.at[i])

    def work(span_of):
        for i in (1, 2, 0):
            weight(i).start()
        for i in span_of:
            fetch(i).start()
        weight(1).wait()
        table_ref[:rows, :] = half_table(nodes_ref[...], weight_buf[1])
        weight(2).wait()
        table_ref[rows:, :] = half_table(nodes_ref[...], weight_buf[2])
        weight(0).wait()
        for i in span_of:
            fetch(i).wait()
            picks = own_picks(send_ref, recv_ref, i * count, count, rows)
            ahead = dot(edges_buf[span(i), :], weight_buf[0]) + bias_ref[layer : layer + 1, :]
            out_buf[span(i), :] = ahead * 0.5 + dot(picks, table_ref[...])
            put(i).start()
        for i in span_of:
            put(i).wait()

    even = lax.axis_index("region") % 2 == 0
    early = steps // 2

    @pl.when(even)
    def _():
        work(range(early, steps) if late else range(early))

    if late:

        @pl.when(jnp.logical_not(even))
        def _():
            work(range(steps))


def edge_kernel(rows, layer, size, *refs):
    valid_ref, owner_ref, send_ref, recv_ref, edges_ref, pre_ref, own_ref = refs[:7]
    near = refs[7:-13]
    far_ref, ws_ref, wr_ref, wo_ref, gain_ref, shift_ref = refs[-13:-7]
    out_ref, to_prev_ref, kept_ref, to_next_ref = refs[-7:-3]
    near_ref, table_ref, total_ref = refs[-3:]
    step = pl.program_id(0)

    @pl.when(step == 0)
    def _():
        for side in range(2):
            near_ref[side * rows : (side + 1) * rows, :] = near[side][...]
        blocks = near_ref[...]
        weight_s = ws_ref[0, 0]
        table_ref[: 2 * rows, :] = half_table(blocks, weight_s)
        table_ref[2 * rows : 4 * rows, :] = half_table(blocks, wr_ref[0, 0])
        away = owner_ref[layer] - lax.axis_index("patch")
        away = jnp.where(away < 0, away + size, away)
        hub = own_ref[:HUB, :]
        if size > 3:
            spot = jnp.clip(away - 2, 0, size - 4)
            hub = jnp.where(away > 1, far_ref[pl.ds(pl.multiple_of(spot * HUB, HUB), HUB), :], hub)
        hub = jnp.where(away == size - 1, near_ref[:HUB, :], hub)
        hub = jnp.where(away == 1, near_ref[rows : rows + HUB, :], hub)
        hub = jnp.where(away == 0, own_ref[:HUB, :], hub)
        table_ref[4 * rows : 4 * rows + HUB, :] = half_table(hub, weight_s)
        table_ref[4 * rows + HUB :, :] = jnp.zeros_like(table_ref[4 * rows + HUB :, :])
        total_ref[...] = jnp.zeros_like(total_ref)

    block = out_ref.shape[0]
    part = min(block, 512)
    count = part // LANES
    first = step * (block // LANES)
    valid = valid_ref[0]
    near_spans, far_spans = [
        tuple((start + at, 2 * LANES) for at in range(0, rows, 2 * LANES)) for start in (0, 2 * rows)
    ]
    hubs = ((3 * rows, LANES),)
    halves = []
    for i in range(block // part):
        at = first + i * count
        picks = jnp.concatenate(
            [
                selector(send_ref, at, count, near_spans + far_spans),
                selector(recv_ref, at, count, near_spans + far_spans),
                selector(send_ref, at, count, hubs),
            ],
            axis=1,
        )
        halves.append(pre_ref[i * part : (i + 1) * part, :] + dot(picks, table_ref[...]))
    updates = []
    for i, half in enumerate(halves):
        mixed = dot(silu_of_half(half).astype(BF16), wo_ref[0])
        normed = layer_norm(mixed, gain_ref[layer : layer + 1, :], shift_ref[layer : layer + 1, :])
        latent = edges_ref[i * part : (i + 1) * part, :].astype(F32)
        updates.append((latent + normed).astype(BF16))
        out_ref[i * part : (i + 1) * part, :] = updates[-1]
    live = selector_rows(recv_ref, first, block // LANES, 3 * rows, valid)
    total_ref[...] += dot(live, jnp.concatenate(updates, axis=0))

    @pl.when((step + 1) * block > valid)
    def _():
        slot = step * block + lax.broadcasted_iota(jnp.int32, (block, 1), 0)
        out_ref[...] = jnp.where(slot < valid, out_ref[...].astype(F32), 0.0).astype(BF16)

    @pl.when(step == pl.num_programs(0) - 1)
    def _():
        to_prev_ref[...] = total_ref[:rows, :].astype(BF16)
        kept_ref[...] = total_ref[rows : 2 * rows, :]
        to_next_ref[...] = total_ref[2 * rows :, :].astype(BF16)


def node_kernel(
    layer,
    nodes_ref,
    kept_ref,
    from_prev_ref,
    from_next_ref,
    wh_ref,
    wa_ref,
    bias_ref,
    wo_ref,
    gain_ref,
    shift_ref,
    *refs,
):
    out_ref = refs[-1]
    nodes = nodes_ref[...]
    summed = from_prev_ref[...].astype(F32) + kept_ref[...] + from_next_ref[...].astype(F32)
    pre_node = dot(nodes, wh_ref[0, 0]) + dot(summed.astype(BF16), wa_ref[0, 0])
    pre_node = pre_node + bias_ref[layer : layer + 1, :]
    mixed = dot(silu_of_half(pre_node * 0.5).astype(BF16), wo_ref[0])
    normed = layer_norm(mixed, gain_ref[layer : layer + 1, :], shift_ref[layer : layer + 1, :])
    out_ref[...] = (nodes.astype(F32) + normed).astype(BF16)


def whole(shape):
    return pl.BlockSpec(shape, lambda *_: (0,) * len(shape))


def picked(shape, spot):
    block = (1,) * len(spot) + shape[len(spot) :]
    index = tuple(spot) + (0,) * (len(shape) - len(spot))
    return pl.BlockSpec(block, lambda *_: index)


def scalars():
    return pl.BlockSpec(memory_space=pltpu.SMEM)


def cost(flops, moved):
    return pl.CostEstimate(flops=flops, bytes_accessed=moved, transcendentals=0)


def local(
    nodes,
    edges,
    senders,
    receivers,
    valid_counts,
    hub_owner,
    edge_in,
    edge_bias,
    edge_out,
    edge_gain,
    edge_shift,
    node_in,
    node_bias,
    node_out,
    node_gain,
    node_shift,
):
    rows, width = nodes.shape
    slots = edges.shape[0]
    size = lax.axis_size("patch")
    block = min(512, slots)
    steps = slots // block
    pair = min(1024, slots)
    by_pair = pl.BlockSpec((pair, width), lambda i: (i, 0))
    send = senders.reshape(slots // LANES, LANES)
    recv = receivers.reshape(slots // LANES, LANES)
    by_block = pl.BlockSpec((block, width), lambda i: (i, 0))
    square = 2 * slots * width * width

    def start_edges(held):
        late = held is not None
        anywhere = pl.BlockSpec(memory_space=pl.ANY)
        given = (held,) if late else ()
        fixed = [
            pltpu.with_memory_space_constraint(value, pltpu.HBM)
            for value in (send, recv, nodes, edge_bias, edges, edge_in)
        ]
        return pl.pallas_call(
            functools.partial(first_kernel, late, 0, steps),
            out_shape=jax.ShapeDtypeStruct((slots, width), F32),
            in_specs=[whole(send.shape), whole(recv.shape), whole(nodes.shape)]
            + [whole(edge_bias.shape), anywhere, anywhere]
            + [anywhere] * len(given),
            out_specs=anywhere,
            grid=(1,),
            input_output_aliases={6: 0} if late else {},
            scratch_shapes=[
                pltpu.VMEM((2 * rows, width), BF16),
                pltpu.VMEM((3, width, width), BF16),
                pltpu.VMEM((slots, width), BF16),
                pltpu.VMEM((slots, width), F32),
                pltpu.SemaphoreType.DMA((3,)),
                pltpu.SemaphoreType.DMA((steps,)),
                pltpu.SemaphoreType.DMA((steps,)),
            ],
            compiler_params=pltpu.CompilerParams(vmem_limit_bytes=GRANT),
            cost_estimate=cost(2 * square, 6 * slots * width),
            name="late_part" if late else "early_part",
        )(*fixed, *given)

    early = start_edges(None)
    sent, early = lax.optimization_barrier((nodes, early))
    for layer in range(LAYERS):
        near = [from_behind(sent, "patch", d) for d in (1, -1)]
        top = sent[:HUB]
        far = [from_behind(top, "patch", -d) for d in range(2, size - 1)]
        far = jnp.concatenate(far, axis=0) if len(far) > 1 else (far[0] if far else top)
        ws = picked(edge_in.shape, (layer, 1))
        wr = picked(edge_in.shape, (layer, 2))
        if layer == 0:
            pre = start_edges(early)
        else:
            pre = pl.pallas_call(
                own_kernel,
                out_shape=jax.ShapeDtypeStruct((slots, width), F32),
                grid=(steps,),
                in_specs=[whole(send.shape), whole(recv.shape), whole(nodes.shape), ws, wr]
                + [by_block],
                out_specs=by_block,
                scratch_shapes=[pltpu.VMEM((2 * rows, width), BF16)],
                compiler_params=pltpu.CompilerParams(vmem_limit_bytes=GRANT),
                cost_estimate=cost(square, 8 * slots * width),
                name="own_part",
            )(send, recv, nodes, edge_in, edge_in, pre)
        edges, to_prev, kept, to_next = pl.pallas_call(
            functools.partial(edge_kernel, rows, layer, size),
            out_shape=(
                jax.ShapeDtypeStruct((slots, width), BF16),
                jax.ShapeDtypeStruct((rows, width), BF16),
                jax.ShapeDtypeStruct((rows, width), F32),
                jax.ShapeDtypeStruct((rows, width), BF16),
            ),
            grid=(slots // pair,),
            in_specs=[
                scalars(),
                scalars(),
                whole(send.shape),
                whole(recv.shape),
                by_pair,
                by_pair,
            ]
            + [whole(nodes.shape)] * (1 + len(near))
            + [
                whole(far.shape),
                ws,
                wr,
                picked(edge_out.shape, (layer,)),
                whole(edge_gain.shape),
                whole(edge_shift.shape),
            ],
            out_specs=(by_pair,) + (whole((rows, width)),) * 3,
            scratch_shapes=[
                pltpu.VMEM((2 * rows, width), BF16),
                pltpu.VMEM((4 * rows + LANES, width), BF16),
                pltpu.VMEM((3 * rows, width), F32),
            ],
            compiler_params=pltpu.CompilerParams(vmem_limit_bytes=GRANT),
            cost_estimate=cost(6 * square, 8 * slots * width),
            name="edge_part",
        )(
            valid_counts,
            hub_owner.reshape(-1),
            send,
            recv,
            edges,
            pre,
            nodes,
            *near,
            far,
            edge_in,
            edge_in,
            edge_out,
            edge_gain,
            edge_shift,
        )
        sum_next = from_behind(to_prev, "patch", -1)
        sum_prev = from_behind(to_next, "patch", 1)
        after = ()
        if layer + 1 < LAYERS:
            pre = pl.pallas_call(
                functools.partial(linear_kernel, layer + 1),
                out_shape=jax.ShapeDtypeStruct((slots, width), F32),
                grid=(steps,),
                in_specs=[
                    by_block,
                    picked(edge_in.shape, (layer + 1, 0)),
                    whole(edge_bias.shape),
                ],
                out_specs=by_block,
                compiler_params=pltpu.CompilerParams(vmem_limit_bytes=GRANT),
                cost_estimate=cost(square, 6 * slots * width),
                name="linear_part",
            )(edges, edge_in, edge_bias)
            after = (pre,)
        nodes = pl.pallas_call(
            functools.partial(node_kernel, layer),
            out_shape=jax.ShapeDtypeStruct((rows, width), BF16),
            grid=(1,),
            in_specs=[whole((rows, width))] * 4
            + [
                picked(node_in.shape, (layer, 0)),
                picked(node_in.shape, (layer, 1)),
                whole(node_bias.shape),
                picked(node_out.shape, (layer,)),
                whole(node_gain.shape),
                whole(node_shift.shape),
            ]
            + [pl.BlockSpec(memory_space=pl.ANY)] * len(after),
            out_specs=whole((rows, width)),
            compiler_params=pltpu.CompilerParams(vmem_limit_bytes=GRANT),
            cost_estimate=cost(6 * rows * width * width, 2 * width * width * 3),
            name="node_part",
        )(
            nodes,
            kept,
            sum_prev,
            sum_next,
            node_in,
            node_in,
            node_bias,
            node_out,
            node_gain,
            node_shift,
            *after,
        )
        sent = nodes
    return (nodes, edges)


def solution(mesh):
    placed = (
        P(("region", "patch"), None),
        P(("region", "patch"), None),
        P(("region", "patch")),
        P(("region", "patch")),
        P(("region", "patch")),
        P(None, "region"),
    ) + (P(),) * 10
    return jax.shard_map(
        local,
        mesh=mesh,
        in_specs=placed,
        out_specs=(P(("region", "patch"), None), P(("region", "patch"), None)),
        check_vma=False,
    )
```

```python
import functools

import jax
import jax.numpy as jnp
from jax import lax
from jax.experimental import pallas as pl
from jax.experimental.pallas import tpu as pltpu
from jax.sharding import PartitionSpec as P


HUB = 32
LAYERS = 2
LANES = 128
GRANT = 24 << 20

epsilon = 1e-05

F32 = jnp.float32
BF16 = jnp.bfloat16


def from_behind(block, axis, distance):
    size = lax.axis_size(axis)
    return lax.ppermute(block, axis, [((i - distance) % size, i) for i in range(size)])


def dot(left, right):
    return jnp.dot(left, right, preferred_element_type=F32)


def silu_of_half(half):
    return half + half * jnp.tanh(half)


def half_table(rows, weight):
    return (dot(rows, weight) * 0.5).astype(BF16)


def layer_norm(value, gain, shift):
    center = value - jnp.mean(value, axis=-1, keepdims=True)
    spread = jnp.mean(center * center, axis=-1, keepdims=True)
    return center * lax.rsqrt(spread + epsilon) * gain + shift


def selector(codes_ref, first, count, starts):
    groups = []
    for i in range(count):
        row = codes_ref[pl.ds(first + i, 1), :]
        parts = []
        for start, width in starts:
            near = jnp.clip(row - start, -1, width).astype(F32)
            near = jnp.broadcast_to(near, (LANES, LANES)).T.astype(BF16)
            for t in range(width // LANES):
                lane = lax.broadcasted_iota(jnp.int32, (LANES, LANES), 1) + t * LANES
                parts.append(jnp.where(near == lane.astype(BF16), BF16(1), BF16(0)))
        groups.append(jnp.concatenate(parts, axis=1))
    return jnp.concatenate(groups, axis=0)


def selector_rows(codes_ref, first, count, width, valid):
    tile = 2 * LANES
    groups = []
    for i in range(count):
        slot = (first + i) * LANES + lax.broadcasted_iota(jnp.int32, (1, LANES), 1)
        row = jnp.where(slot < valid, codes_ref[pl.ds(first + i, 1), :], -1)
        parts = []
        for start in range(0, width, tile):
            near = jnp.clip(row - start, -1, tile).astype(F32)
            near = jnp.broadcast_to(near, (tile, LANES)).astype(BF16)
            sub = lax.broadcasted_iota(jnp.int32, (tile, LANES), 0).astype(BF16)
            parts.append(jnp.where(near == sub, BF16(1), BF16(0)))
        groups.append(jnp.concatenate(parts, axis=0))
    return jnp.concatenate(groups, axis=1)


def linear_kernel(layer, edges_ref, weight_ref, bias_ref, out_ref):
    ahead = dot(edges_ref[...], weight_ref[0, 0]) + bias_ref[layer : layer + 1, :]
    out_ref[...] = ahead * 0.5


def store_kernel(held_ref, out_ref):
    out_ref[...] = held_ref[...]


def own_table(nodes, ws_ref, wr_ref, table_ref):
    rows = nodes.shape[0]
    table_ref[:rows, :] = half_table(nodes, ws_ref[0, 0])
    table_ref[rows:, :] = half_table(nodes, wr_ref[0, 0])


def own_picks(send_ref, recv_ref, first, count, rows):
    spans = tuple((rows + at, 2 * LANES) for at in range(0, rows, 2 * LANES))
    return jnp.concatenate(
        [selector(send_ref, first, count, spans), selector(recv_ref, first, count, spans)],
        axis=1,
    )


def own_sum(step, send_ref, recv_ref, nodes_ref, ws_ref, wr_ref, table_ref, edges):
    rows = nodes_ref.shape[0]

    @pl.when(step == 0)
    def _():
        own_table(nodes_ref[...], ws_ref, wr_ref, table_ref)

    count = edges // LANES
    return dot(own_picks(send_ref, recv_ref, step * count, count, rows), table_ref[...])


def own_kernel(send_ref, recv_ref, nodes_ref, ws_ref, wr_ref, pre_ref, out_ref, table_ref):
    gathered = own_sum(
        pl.program_id(0), send_ref, recv_ref, nodes_ref, ws_ref, wr_ref, table_ref, out_ref.shape[0]
    )
    out_ref[...] = pre_ref[...] + gathered


def first_kernel(late, layer, steps, *refs):
    send_ref, recv_ref, nodes_ref, bias_ref, edges_ref, weights_ref = refs[:6]
    out_ref, table_ref, weight_buf, edges_buf, out_buf, weight_sem, in_sem, out_sem = refs[-8:]
    rows = nodes_ref.shape[0]
    block = edges_buf.shape[0] // steps
    count = block // LANES

    def span(i):
        return pl.ds(i * block, block)

    def fetch(i):
        return pltpu.make_async_copy(edges_ref.at[span(i)], edges_buf.at[span(i)], in_sem.at[i])

    def weight(i):
        return pltpu.make_async_copy(weights_ref.at[layer, i], weight_buf.at[i], weight_sem.at[i])

    def put(i):
        return pltpu.make_async_copy(out_buf.at[span(i)], out_ref.at[span(i)], out_sem.at[i])

    def work(span_of):
        for i in (1, 2, 0):
            weight(i).start()
        for i in span_of:
            fetch(i).start()
        weight(1).wait()
        table_ref[:rows, :] = half_table(nodes_ref[...], weight_buf[1])
        weight(2).wait()
        table_ref[rows:, :] = half_table(nodes_ref[...], weight_buf[2])
        weight(0).wait()
        for i in span_of:
            fetch(i).wait()
            picks = own_picks(send_ref, recv_ref, i * count, count, rows)
            ahead = dot(edges_buf[span(i), :], weight_buf[0]) + bias_ref[layer : layer + 1, :]
            out_buf[span(i), :] = ahead * 0.5 + dot(picks, table_ref[...])
            put(i).start()
        for i in span_of:
            put(i).wait()

    even = lax.axis_index("region") % 2 == 0
    early = steps // 2

    @pl.when(even)
    def _():
        work(range(early, steps) if late else range(early))

    if late:

        @pl.when(jnp.logical_not(even))
        def _():
            work(range(steps))


def edge_kernel(rows, layer, size, *refs):
    valid_ref, owner_ref, send_ref, recv_ref, edges_ref, pre_ref, own_ref = refs[:7]
    near = refs[7:-13]
    far_ref, ws_ref, wr_ref, wo_ref, gain_ref, shift_ref = refs[-13:-7]
    out_ref, to_prev_ref, kept_ref, to_next_ref = refs[-7:-3]
    near_ref, table_ref, total_ref = refs[-3:]
    step = pl.program_id(0)

    @pl.when(step == 0)
    def _():
        for side in range(2):
            near_ref[side * rows : (side + 1) * rows, :] = near[side][...]
        blocks = near_ref[...]
        weight_s = ws_ref[0, 0]
        table_ref[: 2 * rows, :] = half_table(blocks, weight_s)
        table_ref[2 * rows : 4 * rows, :] = half_table(blocks, wr_ref[0, 0])
        away = owner_ref[layer] - lax.axis_index("patch")
        away = jnp.where(away < 0, away + size, away)
        hub = own_ref[:HUB, :]
        if size > 3:
            spot = jnp.clip(away - 2, 0, size - 4)
            hub = jnp.where(away > 1, far_ref[pl.ds(pl.multiple_of(spot * HUB, HUB), HUB), :], hub)
        hub = jnp.where(away == size - 1, near_ref[:HUB, :], hub)
        hub = jnp.where(away == 1, near_ref[rows : rows + HUB, :], hub)
        hub = jnp.where(away == 0, own_ref[:HUB, :], hub)
        table_ref[4 * rows : 4 * rows + HUB, :] = half_table(hub, weight_s)
        table_ref[4 * rows + HUB :, :] = jnp.zeros_like(table_ref[4 * rows + HUB :, :])
        total_ref[...] = jnp.zeros_like(total_ref)

    block = out_ref.shape[0]
    part = min(block, 512)
    count = part // LANES
    first = step * (block // LANES)
    valid = valid_ref[0]
    near_spans, far_spans = [
        tuple((start + at, 2 * LANES) for at in range(0, rows, 2 * LANES)) for start in (0, 2 * rows)
    ]
    hubs = ((3 * rows, LANES),)
    halves = []
    for i in range(block // part):
        at = first + i * count
        picks = jnp.concatenate(
            [
                selector(send_ref, at, count, near_spans + far_spans),
                selector(recv_ref, at, count, near_spans + far_spans),
                selector(send_ref, at, count, hubs),
            ],
            axis=1,
        )
        halves.append(pre_ref[i * part : (i + 1) * part, :] + dot(picks, table_ref[...]))
    updates = []
    for i, half in enumerate(halves):
        mixed = dot(silu_of_half(half).astype(BF16), wo_ref[0])
        normed = layer_norm(mixed, gain_ref[layer : layer + 1, :], shift_ref[layer : layer + 1, :])
        latent = edges_ref[i * part : (i + 1) * part, :].astype(F32)
        updates.append((latent + normed).astype(BF16))
        out_ref[i * part : (i + 1) * part, :] = updates[-1]
    live = selector_rows(recv_ref, first, block // LANES, 3 * rows, valid)
    total_ref[...] += dot(live, jnp.concatenate(updates, axis=0))

    @pl.when((step + 1) * block > valid)
    def _():
        slot = step * block + lax.broadcasted_iota(jnp.int32, (block, 1), 0)
        out_ref[...] = jnp.where(slot < valid, out_ref[...].astype(F32), 0.0).astype(BF16)

    @pl.when(step == pl.num_programs(0) - 1)
    def _():
        to_prev_ref[...] = total_ref[:rows, :].astype(BF16)
        kept_ref[...] = total_ref[rows : 2 * rows, :]
        to_next_ref[...] = total_ref[2 * rows :, :].astype(BF16)


def node_kernel(
    layer,
    nodes_ref,
    kept_ref,
    from_prev_ref,
    from_next_ref,
    wh_ref,
    wa_ref,
    bias_ref,
    wo_ref,
    gain_ref,
    shift_ref,
    *refs,
):
    out_ref = refs[-1]
    nodes = nodes_ref[...]
    summed = from_prev_ref[...].astype(F32) + kept_ref[...] + from_next_ref[...].astype(F32)
    pre_node = dot(nodes, wh_ref[0, 0]) + dot(summed.astype(BF16), wa_ref[0, 0])
    pre_node = pre_node + bias_ref[layer : layer + 1, :]
    mixed = dot(silu_of_half(pre_node * 0.5).astype(BF16), wo_ref[0])
    normed = layer_norm(mixed, gain_ref[layer : layer + 1, :], shift_ref[layer : layer + 1, :])
    out_ref[...] = (nodes.astype(F32) + normed).astype(BF16)


def whole(shape):
    return pl.BlockSpec(shape, lambda *_: (0,) * len(shape))


def picked(shape, spot):
    block = (1,) * len(spot) + shape[len(spot) :]
    index = tuple(spot) + (0,) * (len(shape) - len(spot))
    return pl.BlockSpec(block, lambda *_: index)


def scalars():
    return pl.BlockSpec(memory_space=pltpu.SMEM)


def cost(flops, moved):
    return pl.CostEstimate(flops=flops, bytes_accessed=moved, transcendentals=0)


def local(
    nodes,
    edges,
    senders,
    receivers,
    valid_counts,
    hub_owner,
    edge_in,
    edge_bias,
    edge_out,
    edge_gain,
    edge_shift,
    node_in,
    node_bias,
    node_out,
    node_gain,
    node_shift,
):
    rows, width = nodes.shape
    slots = edges.shape[0]
    size = lax.axis_size("patch")
    block = min(512, slots)
    steps = slots // block
    pair = min(1024, slots)
    by_pair = pl.BlockSpec((pair, width), lambda i: (i, 0))
    send = senders.reshape(slots // LANES, LANES)
    recv = receivers.reshape(slots // LANES, LANES)
    by_block = pl.BlockSpec((block, width), lambda i: (i, 0))
    square = 2 * slots * width * width

    def start_edges(held):
        late = held is not None
        anywhere = pl.BlockSpec(memory_space=pl.ANY)
        given = (held,) if late else ()
        fixed = [
            pltpu.with_memory_space_constraint(value, pltpu.HBM)
            for value in (send, recv, edge_bias, edges, edge_in)
        ]
        around = nodes if late else pltpu.with_memory_space_constraint(nodes, pltpu.HBM)
        return pl.pallas_call(
            functools.partial(first_kernel, late, 0, steps),
            out_shape=jax.ShapeDtypeStruct((slots, width), F32),
            in_specs=[whole(send.shape), whole(recv.shape), whole(nodes.shape)]
            + [whole(edge_bias.shape), anywhere, anywhere]
            + [anywhere] * len(given),
            out_specs=anywhere,
            grid=(1,),
            input_output_aliases={6: 0} if late else {},
            scratch_shapes=[
                pltpu.VMEM((2 * rows, width), BF16),
                pltpu.VMEM((3, width, width), BF16),
                pltpu.VMEM((slots, width), BF16),
                pltpu.VMEM((slots, width), F32),
                pltpu.SemaphoreType.DMA((3,)),
                pltpu.SemaphoreType.DMA((steps,)),
                pltpu.SemaphoreType.DMA((steps,)),
            ],
            compiler_params=pltpu.CompilerParams(vmem_limit_bytes=GRANT),
            cost_estimate=cost(2 * square, 6 * slots * width),
            name="late_part" if late else "early_part",
        )(*fixed[:2], around, *fixed[2:], *given)

    early = start_edges(None)
    sent, early = lax.optimization_barrier((nodes, early))
    for layer in range(LAYERS):
        near = [from_behind(sent, "patch", d) for d in (1, -1)]
        top = sent[:HUB]
        far = [from_behind(top, "patch", -d) for d in range(2, size - 1)]
        far = jnp.concatenate(far, axis=0) if len(far) > 1 else (far[0] if far else top)
        ws = picked(edge_in.shape, (layer, 1))
        wr = picked(edge_in.shape, (layer, 2))
        if layer == 0:
            pre = start_edges(early)
        else:
            pre = pl.pallas_call(
                own_kernel,
                out_shape=jax.ShapeDtypeStruct((slots, width), F32),
                grid=(steps,),
                in_specs=[whole(send.shape), whole(recv.shape), whole(nodes.shape), ws, wr]
                + [by_block],
                out_specs=by_block,
                scratch_shapes=[pltpu.VMEM((2 * rows, width), BF16)],
                compiler_params=pltpu.CompilerParams(vmem_limit_bytes=GRANT),
                cost_estimate=cost(square, 8 * slots * width),
                name="own_part",
            )(send, recv, nodes, edge_in, edge_in, pre)
        edges, to_prev, kept, to_next = pl.pallas_call(
            functools.partial(edge_kernel, rows, layer, size),
            out_shape=(
                jax.ShapeDtypeStruct((slots, width), BF16),
                jax.ShapeDtypeStruct((rows, width), BF16),
                jax.ShapeDtypeStruct((rows, width), F32),
                jax.ShapeDtypeStruct((rows, width), BF16),
            ),
            grid=(slots // pair,),
            in_specs=[
                scalars(),
                scalars(),
                whole(send.shape),
                whole(recv.shape),
                by_pair,
                by_pair,
            ]
            + [whole(nodes.shape)] * (1 + len(near))
            + [
                whole(far.shape),
                ws,
                wr,
                picked(edge_out.shape, (layer,)),
                whole(edge_gain.shape),
                whole(edge_shift.shape),
            ],
            out_specs=(by_pair,) + (whole((rows, width)),) * 3,
            scratch_shapes=[
                pltpu.VMEM((2 * rows, width), BF16),
                pltpu.VMEM((4 * rows + LANES, width), BF16),
                pltpu.VMEM((3 * rows, width), F32),
            ],
            compiler_params=pltpu.CompilerParams(vmem_limit_bytes=GRANT),
            cost_estimate=cost(6 * square, 8 * slots * width),
            name="edge_part",
        )(
            valid_counts,
            hub_owner.reshape(-1),
            send,
            recv,
            edges,
            pre,
            nodes,
            *near,
            far,
            edge_in,
            edge_in,
            edge_out,
            edge_gain,
            edge_shift,
        )
        sum_next = from_behind(to_prev, "patch", -1)
        sum_prev = from_behind(to_next, "patch", 1)
        after = ()
        if layer + 1 < LAYERS:
            pre = pl.pallas_call(
                functools.partial(linear_kernel, layer + 1),
                out_shape=jax.ShapeDtypeStruct((slots, width), F32),
                grid=(steps,),
                in_specs=[
                    by_block,
                    picked(edge_in.shape, (layer + 1, 0)),
                    whole(edge_bias.shape),
                ],
                out_specs=by_block,
                compiler_params=pltpu.CompilerParams(vmem_limit_bytes=GRANT),
                cost_estimate=cost(square, 6 * slots * width),
                name="linear_part",
            )(edges, edge_in, edge_bias)
            after = (pre,)
        else:
            edges = pl.pallas_call(
                store_kernel,
                out_shape=jax.ShapeDtypeStruct((slots, width), BF16),
                grid=(steps,),
                in_specs=[by_block],
                out_specs=by_block,
                compiler_params=pltpu.CompilerParams(vmem_limit_bytes=GRANT),
                cost_estimate=cost(0, 4 * slots * width),
                name="store_part",
            )(edges)
            after = (pltpu.with_memory_space_constraint(edges, pltpu.HBM),)
        nodes = pl.pallas_call(
            functools.partial(node_kernel, layer),
            out_shape=jax.ShapeDtypeStruct((rows, width), BF16),
            grid=(1,),
            in_specs=[whole((rows, width))] * 4
            + [
                picked(node_in.shape, (layer, 0)),
                picked(node_in.shape, (layer, 1)),
                whole(node_bias.shape),
                picked(node_out.shape, (layer,)),
                whole(node_gain.shape),
                whole(node_shift.shape),
            ]
            + [pl.BlockSpec(memory_space=pl.ANY)] * len(after),
            out_specs=whole((rows, width)),
            compiler_params=pltpu.CompilerParams(vmem_limit_bytes=GRANT),
            cost_estimate=cost(6 * rows * width * width, 2 * width * width * 3),
            name="node_part",
        )(
            nodes,
            kept,
            sum_prev,
            sum_next,
            node_in,
            node_in,
            node_bias,
            node_out,
            node_gain,
            node_shift,
            *after,
        )
        sent = nodes
    return (nodes, edges)


def solution(mesh):
    placed = (
        P(("region", "patch"), None),
        P(("region", "patch"), None),
        P(("region", "patch")),
        P(("region", "patch")),
        P(("region", "patch")),
        P(None, "region"),
    ) + (P(),) * 10
    return jax.shard_map(
        local,
        mesh=mesh,
        in_specs=placed,
        out_specs=(P(("region", "patch"), None), P(("region", "patch"), None)),
        check_vma=False,
    )
```

```python
import functools

import jax
import jax.numpy as jnp
from jax import lax
from jax.experimental import pallas as pl
from jax.experimental.pallas import tpu as pltpu
from jax.sharding import PartitionSpec as P


HUB = 32
LAYERS = 2
LANES = 128
GRANT = 24 << 20

epsilon = 1e-05

F32 = jnp.float32
BF16 = jnp.bfloat16


def from_behind(block, axis, distance):
    size = lax.axis_size(axis)
    return lax.ppermute(block, axis, [((i - distance) % size, i) for i in range(size)])


def dot(left, right):
    return jnp.dot(left, right, preferred_element_type=F32)


def silu_of_half(half):
    return half + half * jnp.tanh(half)


def half_table(rows, weight):
    return (dot(rows, weight) * 0.5).astype(BF16)


def layer_norm(value, gain, shift):
    center = value - jnp.mean(value, axis=-1, keepdims=True)
    spread = jnp.mean(center * center, axis=-1, keepdims=True)
    return center * lax.rsqrt(spread + epsilon) * gain + shift


def selector(codes_ref, first, count, starts):
    groups = []
    for i in range(count):
        row = codes_ref[pl.ds(first + i, 1), :]
        parts = []
        for start, width in starts:
            near = jnp.clip(row - start, -1, width).astype(F32)
            near = jnp.broadcast_to(near, (LANES, LANES)).T.astype(BF16)
            for t in range(width // LANES):
                lane = lax.broadcasted_iota(jnp.int32, (LANES, LANES), 1) + t * LANES
                parts.append(jnp.where(near == lane.astype(BF16), BF16(1), BF16(0)))
        groups.append(jnp.concatenate(parts, axis=1))
    return jnp.concatenate(groups, axis=0)


def selector_rows(codes_ref, first, count, width, valid):
    tile = 2 * LANES
    groups = []
    for i in range(count):
        slot = (first + i) * LANES + lax.broadcasted_iota(jnp.int32, (1, LANES), 1)
        row = jnp.where(slot < valid, codes_ref[pl.ds(first + i, 1), :], -1)
        parts = []
        for start in range(0, width, tile):
            near = jnp.clip(row - start, -1, tile).astype(F32)
            near = jnp.broadcast_to(near, (tile, LANES)).astype(BF16)
            sub = lax.broadcasted_iota(jnp.int32, (tile, LANES), 0).astype(BF16)
            parts.append(jnp.where(near == sub, BF16(1), BF16(0)))
        groups.append(jnp.concatenate(parts, axis=0))
    return jnp.concatenate(groups, axis=1)


def linear_kernel(layer, edges_ref, weight_ref, bias_ref, out_ref):
    ahead = dot(edges_ref[...], weight_ref[0, 0]) + bias_ref[layer : layer + 1, :]
    out_ref[...] = ahead * 0.5


def store_kernel(held_ref, out_ref):
    out_ref[...] = held_ref[...]


def own_table(nodes, ws_ref, wr_ref, table_ref):
    rows = nodes.shape[0]
    table_ref[:rows, :] = half_table(nodes, ws_ref[0, 0])
    table_ref[rows:, :] = half_table(nodes, wr_ref[0, 0])


def own_picks(send_ref, recv_ref, first, count, rows):
    spans = tuple((rows + at, 2 * LANES) for at in range(0, rows, 2 * LANES))
    return jnp.concatenate(
        [selector(send_ref, first, count, spans), selector(recv_ref, first, count, spans)],
        axis=1,
    )


def own_sum(step, send_ref, recv_ref, nodes_ref, ws_ref, wr_ref, table_ref, edges):
    rows = nodes_ref.shape[0]

    @pl.when(step == 0)
    def _():
        own_table(nodes_ref[...], ws_ref, wr_ref, table_ref)

    count = edges // LANES
    return dot(own_picks(send_ref, recv_ref, step * count, count, rows), table_ref[...])


def own_kernel(send_ref, recv_ref, nodes_ref, ws_ref, wr_ref, pre_ref, out_ref, table_ref):
    gathered = own_sum(
        pl.program_id(0), send_ref, recv_ref, nodes_ref, ws_ref, wr_ref, table_ref, out_ref.shape[0]
    )
    out_ref[...] = pre_ref[...] + gathered


def first_kernel(late, layer, steps, *refs):
    send_ref, recv_ref, nodes_ref, bias_ref, edges_ref, weights_ref = refs[:6]
    out_ref, table_ref, weight_buf, edges_buf, out_buf, weight_sem, in_sem, out_sem = refs[-8:]
    rows = nodes_ref.shape[0]
    block = edges_buf.shape[0] // steps
    count = block // LANES

    def span(i):
        return pl.ds(i * block, block)

    def fetch(i):
        return pltpu.make_async_copy(edges_ref.at[span(i)], edges_buf.at[span(i)], in_sem.at[i])

    def weight(i):
        return pltpu.make_async_copy(weights_ref.at[layer, i], weight_buf.at[i], weight_sem.at[i])

    def put(i):
        return pltpu.make_async_copy(out_buf.at[span(i)], out_ref.at[span(i)], out_sem.at[i])

    def work(span_of):
        for i in (1, 2, 0):
            weight(i).start()
        for i in span_of:
            fetch(i).start()
        weight(1).wait()
        table_ref[:rows, :] = half_table(nodes_ref[...], weight_buf[1])
        weight(2).wait()
        table_ref[rows:, :] = half_table(nodes_ref[...], weight_buf[2])
        weight(0).wait()
        for i in span_of:
            fetch(i).wait()
            picks = own_picks(send_ref, recv_ref, i * count, count, rows)
            ahead = dot(edges_buf[span(i), :], weight_buf[0]) + bias_ref[layer : layer + 1, :]
            out_buf[span(i), :] = ahead * 0.5 + dot(picks, table_ref[...])
            put(i).start()
        for i in span_of:
            put(i).wait()

    even = lax.axis_index("region") % 2 == 0
    early = steps // 2

    @pl.when(even)
    def _():
        work(range(early, steps) if late else range(early))

    if late:

        @pl.when(jnp.logical_not(even))
        def _():
            work(range(steps))


def edge_kernel(rows, layer, size, *refs):
    valid_ref, owner_ref, send_ref, recv_ref, edges_ref, pre_ref, own_ref = refs[:7]
    near = refs[7:-13]
    far_ref, ws_ref, wr_ref, wo_ref, gain_ref, shift_ref = refs[-13:-7]
    out_ref, to_prev_ref, kept_ref, to_next_ref = refs[-7:-3]
    near_ref, table_ref, total_ref = refs[-3:]
    step = pl.program_id(0)

    @pl.when(step == 0)
    def _():
        for side in range(2):
            near_ref[side * rows : (side + 1) * rows, :] = near[side][...]
        blocks = near_ref[...]
        weight_s = ws_ref[0, 0]
        table_ref[: 2 * rows, :] = half_table(blocks, weight_s)
        table_ref[2 * rows : 4 * rows, :] = half_table(blocks, wr_ref[0, 0])
        away = owner_ref[layer] - lax.axis_index("patch")
        away = jnp.where(away < 0, away + size, away)
        hub = own_ref[:HUB, :]
        if size > 3:
            spot = jnp.clip(away - 2, 0, size - 4)
            hub = jnp.where(away > 1, far_ref[pl.ds(pl.multiple_of(spot * HUB, HUB), HUB), :], hub)
        hub = jnp.where(away == size - 1, near_ref[:HUB, :], hub)
        hub = jnp.where(away == 1, near_ref[rows : rows + HUB, :], hub)
        hub = jnp.where(away == 0, own_ref[:HUB, :], hub)
        table_ref[4 * rows : 4 * rows + HUB, :] = half_table(hub, weight_s)
        table_ref[4 * rows + HUB :, :] = jnp.zeros_like(table_ref[4 * rows + HUB :, :])
        total_ref[...] = jnp.zeros_like(total_ref)

    block = out_ref.shape[0]
    part = min(block, 512)
    count = part // LANES
    first = step * (block // LANES)
    valid = valid_ref[0]
    near_spans, far_spans = [
        tuple((start + at, 2 * LANES) for at in range(0, rows, 2 * LANES)) for start in (0, 2 * rows)
    ]
    hubs = ((3 * rows, LANES),)

    def gathered(i):
        at = first + i * count
        picks = jnp.concatenate(
            [
                selector(send_ref, at, count, near_spans + far_spans),
                selector(recv_ref, at, count, near_spans + far_spans),
                selector(send_ref, at, count, hubs),
            ],
            axis=1,
        )
        return pre_ref[i * part : (i + 1) * part, :] + dot(picks, table_ref[...])

    def mix(half):
        return dot(silu_of_half(half).astype(BF16), wo_ref[0])

    updates = []

    def finish(i, mixed):
        normed = layer_norm(mixed, gain_ref[layer : layer + 1, :], shift_ref[layer : layer + 1, :])
        latent = edges_ref[i * part : (i + 1) * part, :].astype(F32)
        updates.append((latent + normed).astype(BF16))
        out_ref[i * part : (i + 1) * part, :] = updates[-1]

    for i in range(block // part):
        finish(i, mix(gathered(i)))
    live = selector_rows(recv_ref, first, block // LANES, 3 * rows, valid)
    total_ref[...] += dot(live, jnp.concatenate(updates, axis=0))

    @pl.when((step + 1) * block > valid)
    def _():
        slot = step * block + lax.broadcasted_iota(jnp.int32, (block, 1), 0)
        out_ref[...] = jnp.where(slot < valid, out_ref[...].astype(F32), 0.0).astype(BF16)

    @pl.when(step == pl.num_programs(0) - 1)
    def _():
        to_prev_ref[...] = total_ref[:rows, :].astype(BF16)
        kept_ref[...] = total_ref[rows : 2 * rows, :]
        to_next_ref[...] = total_ref[2 * rows :, :].astype(BF16)


def node_kernel(
    layer,
    nodes_ref,
    kept_ref,
    from_prev_ref,
    from_next_ref,
    wh_ref,
    wa_ref,
    bias_ref,
    wo_ref,
    gain_ref,
    shift_ref,
    *refs,
):
    out_ref = refs[-1]
    nodes = nodes_ref[...]
    summed = from_prev_ref[...].astype(F32) + kept_ref[...] + from_next_ref[...].astype(F32)
    pre_node = dot(nodes, wh_ref[0, 0]) + dot(summed.astype(BF16), wa_ref[0, 0])
    pre_node = pre_node + bias_ref[layer : layer + 1, :]
    mixed = dot(silu_of_half(pre_node * 0.5).astype(BF16), wo_ref[0])
    normed = layer_norm(mixed, gain_ref[layer : layer + 1, :], shift_ref[layer : layer + 1, :])
    out_ref[...] = (nodes.astype(F32) + normed).astype(BF16)


def whole(shape):
    return pl.BlockSpec(shape, lambda *_: (0,) * len(shape))


def picked(shape, spot):
    block = (1,) * len(spot) + shape[len(spot) :]
    index = tuple(spot) + (0,) * (len(shape) - len(spot))
    return pl.BlockSpec(block, lambda *_: index)


def scalars():
    return pl.BlockSpec(memory_space=pltpu.SMEM)


def cost(flops, moved):
    return pl.CostEstimate(flops=flops, bytes_accessed=moved, transcendentals=0)


def local(
    nodes,
    edges,
    senders,
    receivers,
    valid_counts,
    hub_owner,
    edge_in,
    edge_bias,
    edge_out,
    edge_gain,
    edge_shift,
    node_in,
    node_bias,
    node_out,
    node_gain,
    node_shift,
):
    rows, width = nodes.shape
    slots = edges.shape[0]
    size = lax.axis_size("patch")
    block = min(512, slots)
    steps = slots // block
    pair = min(2048, slots)
    by_pair = pl.BlockSpec((pair, width), lambda i: (i, 0))
    send = senders.reshape(slots // LANES, LANES)
    recv = receivers.reshape(slots // LANES, LANES)
    by_block = pl.BlockSpec((block, width), lambda i: (i, 0))
    square = 2 * slots * width * width

    def start_edges(held):
        late = held is not None
        anywhere = pl.BlockSpec(memory_space=pl.ANY)
        given = (held,) if late else ()
        fixed = [
            pltpu.with_memory_space_constraint(value, pltpu.HBM)
            for value in (send, recv, edge_bias, edges, edge_in)
        ]
        around = nodes if late else pltpu.with_memory_space_constraint(nodes, pltpu.HBM)
        return pl.pallas_call(
            functools.partial(first_kernel, late, 0, steps),
            out_shape=jax.ShapeDtypeStruct((slots, width), F32),
            in_specs=[whole(send.shape), whole(recv.shape), whole(nodes.shape)]
            + [whole(edge_bias.shape), anywhere, anywhere]
            + [anywhere] * len(given),
            out_specs=anywhere,
            grid=(1,),
            input_output_aliases={6: 0} if late else {},
            scratch_shapes=[
                pltpu.VMEM((2 * rows, width), BF16),
                pltpu.VMEM((3, width, width), BF16),
                pltpu.VMEM((slots, width), BF16),
                pltpu.VMEM((slots, width), F32),
                pltpu.SemaphoreType.DMA((3,)),
                pltpu.SemaphoreType.DMA((steps,)),
                pltpu.SemaphoreType.DMA((steps,)),
            ],
            compiler_params=pltpu.CompilerParams(vmem_limit_bytes=GRANT),
            cost_estimate=cost(2 * square, 6 * slots * width),
            name="late_part" if late else "early_part",
        )(*fixed[:2], around, *fixed[2:], *given)

    early = start_edges(None)
    sent, early = lax.optimization_barrier((nodes, early))
    for layer in range(LAYERS):
        near = [from_behind(sent, "patch", d) for d in (1, -1)]
        top = sent[:HUB]
        far = [from_behind(top, "patch", -d) for d in range(2, size - 1)]
        far = jnp.concatenate(far, axis=0) if len(far) > 1 else (far[0] if far else top)
        ws = picked(edge_in.shape, (layer, 1))
        wr = picked(edge_in.shape, (layer, 2))
        if layer == 0:
            pre = start_edges(early)
        else:
            pre = pl.pallas_call(
                own_kernel,
                out_shape=jax.ShapeDtypeStruct((slots, width), F32),
                grid=(steps,),
                in_specs=[whole(send.shape), whole(recv.shape), whole(nodes.shape), ws, wr]
                + [by_block],
                out_specs=by_block,
                scratch_shapes=[pltpu.VMEM((2 * rows, width), BF16)],
                compiler_params=pltpu.CompilerParams(vmem_limit_bytes=GRANT),
                cost_estimate=cost(square, 8 * slots * width),
                name="own_part",
            )(send, recv, nodes, edge_in, edge_in, pre)
        edges, to_prev, kept, to_next = pl.pallas_call(
            functools.partial(edge_kernel, rows, layer, size),
            out_shape=(
                jax.ShapeDtypeStruct((slots, width), BF16),
                jax.ShapeDtypeStruct((rows, width), BF16),
                jax.ShapeDtypeStruct((rows, width), F32),
                jax.ShapeDtypeStruct((rows, width), BF16),
            ),
            grid=(slots // pair,),
            in_specs=[
                scalars(),
                scalars(),
                whole(send.shape),
                whole(recv.shape),
                by_pair,
                by_pair,
            ]
            + [whole(nodes.shape)] * (1 + len(near))
            + [
                whole(far.shape),
                ws,
                wr,
                picked(edge_out.shape, (layer,)),
                whole(edge_gain.shape),
                whole(edge_shift.shape),
            ],
            out_specs=(by_pair,) + (whole((rows, width)),) * 3,
            scratch_shapes=[
                pltpu.VMEM((2 * rows, width), BF16),
                pltpu.VMEM((4 * rows + LANES, width), BF16),
                pltpu.VMEM((3 * rows, width), F32),
            ],
            compiler_params=pltpu.CompilerParams(vmem_limit_bytes=GRANT),
            cost_estimate=cost(6 * square, 8 * slots * width),
            name="edge_part",
        )(
            valid_counts,
            hub_owner.reshape(-1),
            send,
            recv,
            edges,
            pre,
            nodes,
            *near,
            far,
            edge_in,
            edge_in,
            edge_out,
            edge_gain,
            edge_shift,
        )
        sum_next = from_behind(to_prev, "patch", -1)
        sum_prev = from_behind(to_next, "patch", 1)
        after = ()
        if layer + 1 < LAYERS:
            pre = pl.pallas_call(
                functools.partial(linear_kernel, layer + 1),
                out_shape=jax.ShapeDtypeStruct((slots, width), F32),
                grid=(steps,),
                in_specs=[
                    by_block,
                    picked(edge_in.shape, (layer + 1, 0)),
                    whole(edge_bias.shape),
                ],
                out_specs=by_block,
                compiler_params=pltpu.CompilerParams(vmem_limit_bytes=GRANT),
                cost_estimate=cost(square, 6 * slots * width),
                name="linear_part",
            )(edges, edge_in, edge_bias)
            after = (pre,)
        else:
            edges = pl.pallas_call(
                store_kernel,
                out_shape=jax.ShapeDtypeStruct((slots, width), BF16),
                grid=(steps,),
                in_specs=[by_block],
                out_specs=by_block,
                compiler_params=pltpu.CompilerParams(vmem_limit_bytes=GRANT),
                cost_estimate=cost(0, 4 * slots * width),
                name="store_part",
            )(edges)
            after = (pltpu.with_memory_space_constraint(edges, pltpu.HBM),)
        nodes = pl.pallas_call(
            functools.partial(node_kernel, layer),
            out_shape=jax.ShapeDtypeStruct((rows, width), BF16),
            grid=(1,),
            in_specs=[whole((rows, width))] * 4
            + [
                picked(node_in.shape, (layer, 0)),
                picked(node_in.shape, (layer, 1)),
                whole(node_bias.shape),
                picked(node_out.shape, (layer,)),
                whole(node_gain.shape),
                whole(node_shift.shape),
            ]
            + [pl.BlockSpec(memory_space=pl.ANY)] * len(after),
            out_specs=whole((rows, width)),
            compiler_params=pltpu.CompilerParams(vmem_limit_bytes=GRANT),
            cost_estimate=cost(6 * rows * width * width, 2 * width * width * 3),
            name="node_part",
        )(
            nodes,
            kept,
            sum_prev,
            sum_next,
            node_in,
            node_in,
            node_bias,
            node_out,
            node_gain,
            node_shift,
            *after,
        )
        sent = nodes
    return (nodes, edges)


def solution(mesh):
    placed = (
        P(("region", "patch"), None),
        P(("region", "patch"), None),
        P(("region", "patch")),
        P(("region", "patch")),
        P(("region", "patch")),
        P(None, "region"),
    ) + (P(),) * 10
    return jax.shard_map(
        local,
        mesh=mesh,
        in_specs=placed,
        out_specs=(P(("region", "patch"), None), P(("region", "patch"), None)),
        check_vma=False,
    )
```
